512 devices in a mesh: gx: 64 (over z_lo, y, core), gy: 8 (over x, z_hi).
Axes of the slice: x: 4, y: 8, z: 8 (z_hi: 2, z_lo: 4; z = z_hi * 4 + z_lo), core: 2. Of those that a mesh axis runs over, the one named last changes fastest.
Arguments:
- velocity: float32 [3, 512, 256, 128], P(None, 'gx', 'gy'), may hold values from -6 to 6
- stress: float32 [6, 512, 256, 128], P(None, 'gx', 'gy'), may hold values from -6 to 6
- lame_lambda: bfloat16 [512, 256, 128], P('gx', 'gy'), may hold values from 0.5 to 1.5
- shear_modulus: bfloat16 [512, 256, 128], P('gx', 'gy'), may hold values from 0.29882812 to 1
- buoyancy: bfloat16 [512, 256, 128], P('gx', 'gy'), may hold values from 0.5 to 1.5
- source_p: bfloat16 [3, 512, 256, 128], P(None, 'gx', 'gy'), may hold values from -6 to 6
- source_s: bfloat16 [3, 512, 256, 128], P(None, 'gx', 'gy'), may hold values from -6 to 6
Outputs:
- image_p: float32 [512, 256, 128], P('gx', 'gy')
- image_s: float32 [512, 256, 128], P('gx', 'gy')
The draws below stay inside these ranges and needn't reach their ends.
All inputs are finite; a program needn't handle non-finite values.
Results may differ from the reference program's by a relative error of at most 0.0003.
Values sent between devices are 32-bit elements; how exact they have to be, the bound alone decides.
A program may use at most 64 MiB of HBM per device.

```python
import jax
import jax.numpy as jnp
from jax import lax

NX = 512
NY = 256
NZ = 128
STEPS = 2


def draw_velocity(key, part):
    noise_key = jax.random.fold_in(jax.random.fold_in(key, 11), 0)
    rough = jax.random.normal(noise_key, (3, NX, NY, NZ), jnp.float32)
    return jnp.clip(rough, -6.0, 6.0)


def block_levels(own_key, shape, cuts, least, high):
    gain = 1.0
    for position, shards_of in cuts:
        heights = jax.random.uniform(jax.random.fold_in(jax.random.fold_in(own_key, 6), position), (shards_of,), jnp.float32, least / len(cuts), high / len(cuts))
        gain = gain * jnp.repeat(jnp.exp(heights), shape[position] // shards_of).reshape((-1,) + (1,) * (len(shape) - 1 - position))
    return gain


def centred(stream_key, dims, spread, most, pieces=(), kind=jnp.bfloat16):
    values = jax.random.normal(stream_key, dims, jnp.float32) * spread
    if len(pieces) > 0:
        values = block_levels(stream_key, dims, pieces, -0.22, 0.18) * values
    return jnp.clip(values, min=-most, max=most).astype(kind)


def setup_inputs(seed: int = 0) -> dict:
    key_list = jax.random.split(jax.random.key(seed), 8)
    velocity = draw_velocity(jax.random.fold_in(key_list[7], 71), 0)
    stress = centred(key_list[1], (6, NX, NY, NZ), 1.0, 6.0, ((1, 64), (2, 8)), jnp.float32)
    lame_lambda = jnp.clip(0.5 + 1.0 * jax.random.uniform(key_list[2], (NX, NY, NZ), jnp.float32) ** block_levels(key_list[2], (NX, NY, NZ), ((0, 64), (1, 8)), -0.2, 0.2), 0.5, 1.5).astype(jnp.bfloat16)
    shear_modulus = jnp.clip(0.29882812 + 0.7011719 * jax.random.uniform(key_list[3], (NX, NY, NZ), jnp.float32) ** block_levels(key_list[3], (NX, NY, NZ), ((0, 64), (1, 8)), -0.2, 0.2), 0.29882812, 1.0).astype(jnp.bfloat16)
    buoyancy = jnp.clip(0.5 + 1.0 * jax.random.uniform(key_list[4], (NX, NY, NZ), jnp.float32) ** block_levels(key_list[4], (NX, NY, NZ), ((0, 64), (1, 8)), -0.2, 0.2), 0.5, 1.5).astype(jnp.bfloat16)
    source_p = centred(key_list[5], (3, NX, NY, NZ), 1.0, 6.0, ((1, 64), (2, 8)))
    source_s = centred(key_list[6], (3, NX, NY, NZ), 1.0, 6.0, ((1, 64), (2, 8)))
    return {"velocity": velocity, "stress": stress, "lame_lambda": lame_lambda, "shear_modulus": shear_modulus, "buoyancy": buoyancy, "source_p": source_p, "source_s": source_s}


time_step = 0.2


def next_cell(field, which):
    length = field.shape[which]
    zero_rim = jnp.zeros_like(lax.slice_in_dim(field, 0, 1, axis=which))
    return jnp.concatenate([lax.slice_in_dim(field, 1, length, axis=which), zero_rim], axis=which)


def prior_cell(field, which):
    length = field.shape[which]
    zero_rim = jnp.zeros_like(lax.slice_in_dim(field, 0, 1, axis=which))
    return jnp.concatenate([zero_rim, lax.slice_in_dim(field, 0, length - 1, axis=which)], axis=which)


def stress_update(velocity, stress, lame_value, shear_value):
    x_speed, y_speed, z_speed = velocity[0], velocity[1], velocity[2]
    strain_x = x_speed - prior_cell(x_speed, 0)
    strain_y = y_speed - prior_cell(y_speed, 1)
    strain_z = z_speed - prior_cell(z_speed, 2)
    volume = strain_x + strain_y + strain_z
    normal_x = stress[0] + time_step * (lame_value * volume + 2.0 * shear_value * strain_x)
    normal_y = stress[1] + time_step * (lame_value * volume + 2.0 * shear_value * strain_y)
    normal_z = stress[2] + time_step * (lame_value * volume + 2.0 * shear_value * strain_z)
    shear_xy = stress[3] + time_step * shear_value * ((next_cell(x_speed, 1) - x_speed) + (next_cell(y_speed, 0) - y_speed))
    shear_xz = stress[4] + time_step * shear_value * ((next_cell(x_speed, 2) - x_speed) + (next_cell(z_speed, 0) - z_speed))
    shear_yz = stress[5] + time_step * shear_value * ((next_cell(y_speed, 2) - y_speed) + (next_cell(z_speed, 1) - z_speed))
    return jnp.stack([normal_x, normal_y, normal_z, shear_xy, shear_xz, shear_yz])


def velocity_update(velocity, stress, buoy_value):
    normal_x, normal_y, normal_z = stress[0], stress[1], stress[2]
    shear_xy, shear_xz, shear_yz = stress[3], stress[4], stress[5]
    x_speed = velocity[0] + time_step * buoy_value * ((next_cell(normal_x, 0) - normal_x) + (shear_xy - prior_cell(shear_xy, 1)) + (shear_xz - prior_cell(shear_xz, 2)))
    y_speed = velocity[1] + time_step * buoy_value * ((shear_xy - prior_cell(shear_xy, 0)) + (next_cell(normal_y, 1) - normal_y) + (shear_yz - prior_cell(shear_yz, 2)))
    z_speed = velocity[2] + time_step * buoy_value * ((shear_xz - prior_cell(shear_xz, 0)) + (shear_yz - prior_cell(shear_yz, 1)) + (next_cell(normal_z, 2) - normal_z))
    return jnp.stack([x_speed, y_speed, z_speed])


def signed_index(positions, length):
    half_length = length // 2
    signed = jnp.where(positions < half_length, positions, jnp.where(positions == half_length, 0, positions - length))
    return signed.astype(jnp.float32)


def reference(velocity, stress, lame_lambda, shear_modulus, buoyancy, source_p, source_s):
    lame_value = lame_lambda.astype(jnp.float32)
    shear_value = shear_modulus.astype(jnp.float32)
    buoy_value = buoyancy.astype(jnp.float32)
    for step_index in range(STEPS):
        stress = stress_update(velocity, stress, lame_value, shear_value)
        velocity = velocity_update(velocity, stress, buoy_value)
    spectra = jnp.fft.fftn(velocity, axes=(1, 2, 3))
    wave_x = signed_index(jnp.arange(NX, dtype=jnp.int32), NX)[:, None, None]
    wave_y = signed_index(jnp.arange(NY, dtype=jnp.int32), NY)[None, :, None]
    wave_z = signed_index(jnp.arange(NZ, dtype=jnp.int32), NZ)[None, None, :]
    inverse_norm = 1.0 / jnp.maximum(wave_x * wave_x + wave_y * wave_y + wave_z * wave_z, 1.0)
    radial = (wave_x * spectra[0] + wave_y * spectra[1] + wave_z * spectra[2]) * inverse_norm
    compression = jnp.stack([wave_x * radial, wave_y * radial, wave_z * radial])
    p_field = jnp.real(jnp.fft.ifftn(compression, axes=(1, 2, 3))).astype(jnp.float32)
    s_field = jnp.real(jnp.fft.ifftn(spectra - compression, axes=(1, 2, 3))).astype(jnp.float32)
    image_p = jnp.sum(source_p.astype(jnp.float32) * p_field, axis=0)
    image_s = jnp.sum(source_s.astype(jnp.float32) * s_field, axis=0)
    return image_p, image_s
```

```python
import functools
import math

import jax
import jax.numpy as jnp
import numpy as np
from jax import lax
from jax.experimental import pallas as pl
from jax.experimental.pallas import tpu as pltpu
from jax.sharding import PartitionSpec as P

STEPS = 2
NX, NY, NZ = 512, 256, 128
GX, GY = 64, 8
XL, YL = NX // GX, NY // GY
ROWS = XL * YL
time_step = 0.2

MESH = pl.DeviceIdType.MESH
F32, BF16 = jnp.float32, jnp.bfloat16


def real_form(matrix):
    return np.block([[matrix.real, matrix.imag], [-matrix.imag, matrix.real]])


def left_form(matrix):
    return np.block([[matrix.real, -matrix.imag], [matrix.imag, matrix.real]])


def dft(length, sign):
    k = np.arange(length)
    return np.exp(sign * 2j * math.pi * (np.outer(k, k) % length) / length)


def tables():
    z = np.arange(NZ)
    per = NZ // 2 // GY
    forward_z = np.zeros((NZ, NZ))
    weighted_z = np.zeros((NZ, NZ))
    back_z = np.zeros((NZ, NZ))
    weighted_back = np.zeros((NZ, NZ))
    norm = 1.0 / (NX * NY * NZ)
    for column in range(NZ // 2):
        real_row = (column // per) * 2 * per + column % per
        imag_row = real_row + per
        angle = 2 * math.pi * (column * z % NZ) / NZ
        cosine, sine = np.cos(angle), np.sin(angle)
        if column == 0:
            sign = 1.0 - 2.0 * (z % 2)
            forward_z[real_row], forward_z[imag_row] = 1.0, sign
            back_z[real_row], back_z[imag_row] = norm, norm * sign
        else:
            forward_z[real_row], forward_z[imag_row] = cosine, -sine
            back_z[real_row], back_z[imag_row] = 2 * norm * cosine, -2 * norm * sine
        weighted_z[real_row] = column * forward_z[real_row]
        weighted_z[imag_row] = column * forward_z[imag_row]
        weighted_back[real_row] = column * back_z[real_row]
        weighted_back[imag_row] = column * back_z[imag_row]

    device_y = np.kron(dft(GY, -1), np.eye(per))
    arrive = np.zeros((NZ, NZ))
    for source in range(GY):
        for part in range(2):
            for j in range(per):
                arrive[part * 64 + source * per + j, source * 2 * per + part * per + j] = 1.0
    left_y = left_form(device_y) @ arrive
    left_y_back = arrive.T @ left_form(device_y.conj())
    q1 = np.arange(64) // per
    yl = np.arange(ROWS) % YL
    turn_y = np.exp(-2j * math.pi * (np.outer(q1, yl) % NY) / NY)
    local_y = real_form(np.kron(np.eye(4), dft(YL, -1)))
    local_y_back = real_form(np.kron(np.eye(4), dft(YL, 1)))

    left_x = left_form(dft(GX, -1))
    left_x_back = left_form(dft(GX, 1))
    xl = np.arange(ROWS) // YL
    turn_x = np.exp(-2j * math.pi * (np.outer(np.arange(64), xl) % NX) / NX)
    local_x = []
    for a in range(2):
        small = np.diag(np.exp(-2j * math.pi * a * np.arange(4) / 8)) @ dft(4, -1)
        local_x.append(np.kron(small, np.eye(YL)))
    local_x_back = [real_form(m.conj().T) for m in local_x]
    local_x = [real_form(m) for m in local_x]

    def pair(stack):
        stack = np.stack(stack).astype(np.float32)
        high = stack.astype(BF16)
        low = (stack - high.astype(np.float32)).astype(BF16)
        return np.stack([high, low], axis=1)

    small = pair(
        [forward_z, weighted_z, left_y, left_y_back, left_x, left_x_back, back_z, weighted_back]
    )
    large = pair([local_y, local_y_back] + local_x + local_x_back)
    turns = np.stack([turn_y.real, turn_y.imag, turn_x.real, turn_x.imag]).astype(np.float32)
    return small, large, turns


def split(value):
    high = value.astype(BF16)
    return high, (value - high.astype(F32)).astype(BF16)


def product(left, right, dims):
    def one(a, b):
        return lax.dot_general(a, b, (dims, ((), ())), preferred_element_type=F32)

    return one(left[0], right[0]) + (one(left[0], right[1]) + one(left[1], right[0]))


NN = ((1,), (0,))
NT = ((1,), (1,))
TN = ((0,), (0,))


def matmul(left, right, dims=NN):
    left = left if isinstance(left, tuple) else split(left)
    right = right if isinstance(right, tuple) else split(right)
    return product(left, right, dims)


def turned(real, imag, cosine, sine, back):
    if back:
        return real * cosine + imag * sine, imag * cosine - real * sine
    return real * cosine - imag * sine, imag * cosine + real * sine


def lanes(value, half):
    return value[:, half * 128 : half * 128 + 128]


def z_forward(field, table):
    return matmul(table, field, NT)


def y_forward_left(arrived, left, cosine, sine):
    both = matmul(left, arrived)
    return turned(both[:64], both[64:], cosine, sine, False)


def halves_product(pairs, table):
    stacked = jnp.concatenate(
        [
            jnp.concatenate([lanes(re, h), lanes(im, h)], axis=1)
            for re, im in pairs
            for h in range(2)
        ],
        axis=0,
    )
    out = matmul(stacked, table)
    result = []
    for n in range(len(pairs)):
        rows = [out[(2 * n + h) * 64 : (2 * n + h) * 64 + 64] for h in range(2)]
        result.append(
            tuple(
                jnp.concatenate([r[:, part * 128 : part * 128 + 128] for r in rows], axis=1)
                for part in range(2)
            )
        )
    return result


def signed(positions, length):
    half = length // 2
    value = jnp.where(positions < half, positions, positions - length)
    return jnp.where(positions == half, 0, value).astype(F32)


def iota(axis):
    return lax.broadcasted_iota(jnp.int32, (64, 256), axis)


def wave_y_rows():
    return signed(iota(0) // 8 + 8 * (iota(1) % YL), NY)


def waves_here(gx, gy):
    lane = iota(1)
    k2 = lane // 128 + 2 * (lane % 128 // YL)
    wave_x = signed(iota(0) + 64 * k2, NX)
    wave_y = signed(gx // 8 + 8 * (lane % YL), NY)
    wave_z = (gy * 8 + gx % 8).astype(F32)
    size = wave_x * wave_x + wave_y * wave_y + wave_z * wave_z
    return wave_x, 1.0 / jnp.maximum(size, 1.0)


def x_stage(planes, left, left_back, local, local_back, cosine, sine, wave_x, inverse):
    stacked = jnp.concatenate(
        [
            jnp.concatenate([planes[2 * f][h], planes[2 * f + 1][h]], axis=0)
            for f in range(2)
            for h in range(2)
        ],
        axis=1,
    )
    out = matmul(left, stacked)
    fields = []
    for f in range(2):
        re, im = out[:64, f * 256 : f * 256 + 256], out[64:, f * 256 : f * 256 + 256]
        fields.append(turned(re, im, cosine, sine, False))
    spectra = [[], []]
    for a in range(2):
        rows = []
        for re, im in fields:
            if a == 0:
                re, im = lanes(re, 0) + lanes(re, 1), lanes(im, 0) + lanes(im, 1)
            else:
                re, im = lanes(re, 0) - lanes(re, 1), lanes(im, 0) - lanes(im, 1)
            rows.append(jnp.concatenate([re, im], axis=1))
        got = matmul(jnp.concatenate(rows, axis=0), local[a])
        wave = lanes(wave_x, a)
        scale = lanes(inverse, a)
        phi_re = (wave * got[:64, :128] + got[64:, :128]) * scale
        phi_im = (wave * got[:64, 128:] + got[64:, 128:]) * scale
        both = jnp.concatenate(
            [
                jnp.concatenate([wave * phi_re, wave * phi_im], axis=1),
                jnp.concatenate([phi_re, phi_im], axis=1),
            ],
            axis=0,
        )
        back = matmul(both, local_back[a])
        for f in range(2):
            spectra[a].append((back[f * 64 : f * 64 + 64, :128], back[f * 64 : f * 64 + 64, 128:]))
    stacked = []
    for f in range(2):
        zero, one = spectra[0][f], spectra[1][f]
        for h in range(2):
            if h == 0:
                re, im = zero[0] + one[0], zero[1] + one[1]
            else:
                re, im = zero[0] - one[0], zero[1] - one[1]
            re, im = turned(re, im, lanes(cosine, h), lanes(sine, h), True)
            stacked.append(jnp.concatenate([re, im], axis=0))
    out = matmul(left_back, jnp.concatenate(stacked, axis=1))
    result = []
    for f in range(2):
        for part in range(2):
            rows = out[part * 64 : part * 64 + 64]
            result.append(
                [rows[:, (2 * f + h) * 128 : (2 * f + h) * 128 + 128] for h in range(2)]
            )
    return result


def y_back_left(pair, left, cosine, sine):
    re, im = turned(pair[0], pair[1], cosine, sine, True)
    return matmul(left, jnp.concatenate([re, im], axis=0))


def z_back(arrived, table):
    return matmul(arrived, table, TN)


def kernel(
    velocity, stress, lame, shear, buoy, source_p, source_s, small, large, turns,
    image_p, image_s,
    v_0, v_1, v_2, s_0, s_1, s_2, lame_v, shear_v, buoy_v, source_p_v, source_s_v,
    small_v, large_v, turns_v, y_send, y_recv,
    z_send, z_recv, x_send, x_recv, x_send_2, x_recv_2, z_send_2, z_recv_2,
    load_sem, own_sem, halo_send, halo_recv, gy_send, gy_recv, gx_send, gx_recv,
):
    gx, gy = lax.axis_index("gx"), lax.axis_index("gy")

    def interior(ref):
        return ref.at[:, pl.ds(YL, ROWS)]

    loads = [
        (velocity, interior(v_0)),
        (stress, s_0),
        (lame, lame_v),
        (shear, shear_v),
        (buoy, buoy_v),
        (small, small_v),
        (large, large_v),
        (turns, turns_v),
        (source_p, source_p_v),
        (source_s, source_s_v),
    ]
    loads = [pltpu.make_async_copy(a, b, load_sem.at[n]) for n, (a, b) in enumerate(loads)]
    for load in loads:
        load.start()

    barrier = pltpu.get_barrier_semaphore()

    def greet_x(k, carry):
        pl.semaphore_signal(
            barrier, inc=1, device_id=(lax.rem(gx + k, GX), gy), device_id_type=MESH
        )
        return carry

    def greet_y(k, carry):
        pl.semaphore_signal(
            barrier, inc=1, device_id=(gx, lax.rem(gy + k, GY)), device_id_type=MESH
        )
        return carry

    lax.fori_loop(1, GX, greet_x, 0)
    lax.fori_loop(1, GY, greet_y, 0)
    pl.semaphore_wait(barrier, GX + GY - 2)

    right_x, left_x = (lax.rem(gx + 1, GX), gy), (lax.rem(gx + GX - 1, GX), gy)
    right_y, left_y = (gx, lax.rem(gy + 1, GY)), (gx, lax.rem(gy + GY - 1, GY))

    def send(source, target, device, send_sem, recv_sem):
        copy = pltpu.make_async_remote_copy(
            src_ref=source,
            dst_ref=target,
            send_sem=send_sem,
            recv_sem=recv_sem,
            device_id=device,
            device_id_type=MESH,
        )
        copy.start()
        return copy

    first, last = pl.ds(YL, YL), pl.ds(ROWS, YL)
    below, above = pl.ds(0, YL), pl.ds(ROWS + YL, YL)
    top_rows = pl.ds(YL, XL, stride=YL)
    end_rows = pl.ds(2 * YL - 1, XL, stride=YL)

    def exchange(ref, turn, x_prior, x_next, y_prior, y_next):
        slot = 0
        for field in y_prior:
            y_send[turn, slot] = ref[field, end_rows, :]
            slot += 1
        for field in y_next:
            y_send[turn, slot] = ref[field, top_rows, :]
            slot += 1
        low, high = pl.ds(0, len(y_prior)), pl.ds(len(y_prior), len(y_next))
        a, b = pl.ds(*x_prior), pl.ds(*x_next)
        plan = [
            (y_send.at[turn, low], y_recv.at[turn, low], right_y),
            (y_send.at[turn, high], y_recv.at[turn, high], left_y),
            (ref.at[a, last], ref.at[a, below], right_x),
            (ref.at[b, first], ref.at[b, above], left_x),
        ]
        copies = [
            send(source, target, device, halo_send.at[turn, n], halo_recv.at[turn, n])
            for n, (source, target, device) in enumerate(plan)
        ]
        for copy in copies:
            copy.wait()

        @pl.when(gx == 0)
        def _():
            for n in range(x_prior[1]):
                ref[x_prior[0] + n, below, :] = jnp.zeros((YL, NZ), F32)

        @pl.when(gx == GX - 1)
        def _():
            for n in range(x_next[1]):
                ref[x_next[0] + n, above, :] = jnp.zeros((YL, NZ), F32)

        @pl.when(gy == 0)
        def _():
            for n in range(len(y_prior)):
                y_recv[turn, n] = jnp.zeros((XL, NZ), F32)

        @pl.when(gy == GY - 1)
        def _():
            for n in range(len(y_next)):
                y_recv[turn, len(y_prior) + n] = jnp.zeros((XL, NZ), F32)

    z_lane = lax.broadcasted_iota(jnp.int32, (YL, NZ), 1)
    y_row = lax.broadcasted_iota(jnp.int32, (YL, NZ), 0)

    def next_z(f):
        return jnp.where(z_lane == NZ - 1, 0.0, pltpu.roll(f, NZ - 1, 1))

    def prior_z(f):
        return jnp.where(z_lane == 0, 0.0, pltpu.roll(f, 1, 1))

    def next_y(f, rim):
        return jnp.where(y_row == YL - 1, rim, pltpu.roll(f, YL - 1, 0))

    def prior_y(f, rim):
        return jnp.where(y_row == 0, rim, pltpu.roll(f, 1, 0))

    def stress_update(v, s_in, s_in_base, s_out, turn):
        def plane(i, carry):
            here = pl.ds(pl.multiple_of((i + 1) * YL, YL), YL)
            before = pl.ds(pl.multiple_of(i * YL, YL), YL)
            after = pl.ds(pl.multiple_of((i + 2) * YL, YL), YL)
            inner = pl.ds(pl.multiple_of(i * YL, YL), YL)
            old = pl.ds(pl.multiple_of(i * YL + s_in_base, YL), YL)

            def rim(n):
                return y_recv[turn, n, pl.ds(i, 1), :]

            v_x, v_y, v_z = v[0, here, :], v[1, here, :], v[2, here, :]
            lam = lame_v[inner, :].astype(F32) * time_step
            mu = shear_v[inner, :].astype(F32) * time_step
            e_x = v_x - v[0, before, :]
            e_y = v_y - prior_y(v_y, rim(0))
            e_z = v_z - prior_z(v_z)
            volume = lam * (e_x + e_y + e_z)
            twice = 2.0 * mu
            s_out[0, here, :] = s_in[0, old, :] + (volume + twice * e_x)
            s_out[1, here, :] = s_in[1, old, :] + (volume + twice * e_y)
            s_out[2, here, :] = s_in[2, old, :] + (volume + twice * e_z)
            s_out[3, here, :] = s_in[3, old, :] + mu * (
                (next_y(v_x, rim(1)) - v_x) + (v[1, after, :] - v_y)
            )
            s_out[4, here, :] = s_in[4, old, :] + mu * (
                (next_z(v_x) - v_x) + (v[2, after, :] - v_z)
            )
            s_out[5, here, :] = s_in[5, old, :] + mu * (
                (next_z(v_y) - v_y) + (next_y(v_z, rim(2)) - v_z)
            )
            return carry

        lax.fori_loop(0, XL, plane, 0)

    def velocity_update(v_in, s, v_out, turn):
        def plane(i, carry):
            here = pl.ds(pl.multiple_of((i + 1) * YL, YL), YL)
            before = pl.ds(pl.multiple_of(i * YL, YL), YL)
            after = pl.ds(pl.multiple_of((i + 2) * YL, YL), YL)
            inner = pl.ds(pl.multiple_of(i * YL, YL), YL)

            def rim(n):
                return y_recv[turn, n, pl.ds(i, 1), :]

            b = buoy_v[inner, :].astype(F32) * time_step
            xx, yy, zz = s[0, here, :], s[1, here, :], s[2, here, :]
            xy, xz, yz = s[3, here, :], s[4, here, :], s[5, here, :]
            v_out[0, here, :] = v_in[0, here, :] + b * (
                (s[0, after, :] - xx) + (xy - prior_y(xy, rim(0))) + (xz - prior_z(xz))
            )
            v_out[1, here, :] = v_in[1, here, :] + b * (
                (xy - s[3, before, :]) + (next_y(yy, rim(2)) - yy) + (yz - prior_z(yz))
            )
            v_out[2, here, :] = v_in[2, here, :] + b * (
                (xz - s[4, before, :]) + (yz - prior_y(yz, rim(1))) + (next_z(zz) - zz)
            )
            return carry

        lax.fori_loop(0, XL, plane, 0)

    loads[0].wait()
    exchange(v_0, 0, (0, 1), (1, 2), [1], [0, 2])
    for load in loads[1:4]:
        load.wait()
    stress_update(v_0, s_0, 0, s_1, 0)
    exchange(s_1, 1, (3, 2), (0, 1), [3, 5], [1])
    loads[4].wait()
    velocity_update(v_0, s_1, v_1, 1)
    exchange(v_1, 2, (0, 1), (1, 2), [1], [0, 2])
    stress_update(v_1, s_1, YL, s_2, 2)
    exchange(s_2, 3, (3, 2), (0, 1), [3, 5], [1])
    velocity_update(v_1, s_2, v_2, 3)

    for load in loads[5:8]:
        load.wait()

    def narrow(n):
        return small_v[n, 0], small_v[n, 1]

    def wide(n):
        return large_v[n, 0], large_v[n, 1]

    def all_to_all_gy(field, sent, received, turn):
        mine = pl.ds(pl.multiple_of(gy * 16, 16), 16)

        def one(k, carry):
            to = lax.rem(gy + k, GY)
            send(
                sent.at[field, pl.ds(pl.multiple_of(to * 16, 16), 16)],
                received.at[field, mine],
                (gx, to),
                gy_send.at[turn, field],
                gy_recv.at[turn, field],
            )
            return carry

        lax.fori_loop(1, GY, one, 0)
        received[field, mine, :] = sent[field, mine, :]

    def wait_gy(field, received, sems, turn):
        part = received.at[field, pl.ds(0, 16 * (GY - 1))]
        pltpu.make_async_copy(part, part, sems.at[turn, field]).wait()

    def all_to_all_gx(sent, received, turn):
        mine = pl.ds(pl.multiple_of(gx * 8, 8), 8)

        def one(k, carry):
            to = lax.rem(gx + k, GX)
            send(
                sent.at[pl.ds(pl.multiple_of(to * 8, 8), 8)],
                received.at[mine],
                (to, gy),
                gx_send.at[turn],
                gx_recv.at[turn],
            )
            return carry

        lax.fori_loop(1, GX, one, 0)
        received[mine, :] = sent[mine, :]

    def wait_gx(received, sems, turn):
        part = received.at[pl.ds(0, 8 * (GX - 1))]
        pltpu.make_async_copy(part, part, sems.at[turn]).wait()

    turn_y = turns_v[0], turns_v[1]
    turn_x = turns_v[2], turns_v[3]

    for field in range(3):
        table = narrow(1 if field == 2 else 0)
        z_send[field] = z_forward(v_2[field, pl.ds(YL, ROWS), :], table)
        all_to_all_gy(field, z_send, z_recv, 0)

    pairs = []
    for field in range(3):
        wait_gy(field, z_recv, gy_recv, 0)
        pairs.append(y_forward_left(z_recv[field], narrow(2), *turn_y))
    pairs = halves_product(pairs, wide(0))
    wave_y = wave_y_rows()
    joined = [wave_y * pairs[1][part] + pairs[2][part] for part in range(2)]
    for p, value in enumerate([pairs[0][0], pairs[0][1]] + joined):
        for h in range(2):
            x_send[pl.ds(2 * p + h, 64, stride=8), :] = lanes(value, h)
    all_to_all_gx(x_send, x_recv, 0)

    wave_x, inverse = waves_here(gx, gy)
    wait_gx(x_recv, gx_recv, 0)
    planes = [[x_recv[pl.ds(2 * p + h, 64, stride=8), :] for h in range(2)] for p in range(4)]
    planes = x_stage(
        planes,
        narrow(4),
        narrow(5),
        [wide(2), wide(3)],
        [wide(4), wide(5)],
        *turn_x,
        wave_x,
        inverse,
    )
    for p in range(4):
        for h in range(2):
            x_send_2[pl.ds(2 * p + h, 64, stride=8), :] = planes[p][h]
    all_to_all_gx(x_send_2, x_recv_2, 1)

    wait_gx(x_recv_2, gx_recv, 1)
    planes = [
        jnp.concatenate([x_recv_2[pl.ds(2 * p + h, 64, stride=8), :] for h in range(2)], axis=1)
        for p in range(4)
    ]
    pairs = [
        (planes[0], planes[1]),
        (wave_y * planes[2], wave_y * planes[3]),
        (planes[2], planes[3]),
    ]
    pairs = halves_product(pairs, wide(1))
    for field in range(3):
        z_send_2[field] = y_back_left(pairs[field], narrow(3), *turn_y)
        all_to_all_gy(field, z_send_2, z_recv_2, 1)

    for load in loads[8:]:
        load.wait()
    total_p = jnp.zeros((ROWS, NZ), F32)
    total_s = jnp.zeros((ROWS, NZ), F32)
    for field in range(3):
        wait_gy(field, z_recv_2, gy_recv, 1)
        p_field = z_back(z_recv_2[field], narrow(7 if field == 2 else 6))
        s_field = v_2[field, pl.ds(YL, ROWS), :] - p_field
        total_p += source_p_v[field].astype(F32) * p_field
        total_s += source_s_v[field].astype(F32) * s_field
    image_p[...] = total_p
    image_s[...] = total_s

    for field in range(3):
        wait_gy(field, z_send, gy_send, 0)
        wait_gy(field, z_send_2, gy_send, 1)
    wait_gx(x_send, gx_send, 0)
    wait_gx(x_send_2, gx_send, 1)


def shards(small, large, turns, velocity, stress, lame, shear, buoy, source_p, source_s):
    any_space = pl.BlockSpec(memory_space=pl.ANY)
    padded = (XL + 2) * YL
    dma = pltpu.SemaphoreType.DMA
    scratch = [
        *[pltpu.VMEM((3, padded, NZ), F32)] * 3,
        pltpu.VMEM((6, ROWS, NZ), F32),
        *[pltpu.VMEM((6, padded, NZ), F32)] * 2,
        *[pltpu.VMEM((ROWS, NZ), BF16)] * 3,
        *[pltpu.VMEM((3, ROWS, NZ), BF16)] * 2,
        pltpu.VMEM(small.shape, BF16),
        pltpu.VMEM(large.shape, BF16),
        pltpu.VMEM(turns.shape, F32),
        *[pltpu.VMEM((4, 3, XL, NZ), F32)] * 2,
        *[pltpu.VMEM((3, NZ, ROWS), F32)] * 2,
        *[pltpu.VMEM((8 * GX, NZ), F32)] * 4,
        *[pltpu.VMEM((3, NZ, ROWS), F32)] * 2,
        dma((10,)),
        dma((1,)),
        dma((4, 4)),
        dma((4, 4)),
        dma((2, 3)),
        dma((2, 3)),
        dma((2,)),
        dma((2,)),
    ]
    out = jax.ShapeDtypeStruct((ROWS, NZ), F32)
    outs = pl.pallas_call(
        kernel,
        out_shape=(out, out),
        in_specs=[any_space] * 10,
        out_specs=(pl.BlockSpec(memory_space=pltpu.VMEM),) * 2,
        scratch_shapes=scratch,
        compiler_params=pltpu.CompilerParams(
            collective_id=0, has_side_effects=True, vmem_limit_bytes=40 * 2**20
        ),
    )(
        velocity.reshape(3, ROWS, NZ),
        stress.reshape(6, ROWS, NZ),
        lame.reshape(ROWS, NZ),
        shear.reshape(ROWS, NZ),
        buoy.reshape(ROWS, NZ),
        source_p.reshape(3, ROWS, NZ),
        source_s.reshape(3, ROWS, NZ),
        small,
        large,
        turns,
    )
    return tuple(o.reshape(XL, YL, NZ) for o in outs)


def solution(mesh):
    small, large, turns = tables()

    def body(*blocks):
        return shards(jnp.asarray(small), jnp.asarray(large), jnp.asarray(turns), *blocks)

    in_specs = (
        P(None, "gx", "gy", None),
        P(None, "gx", "gy", None),
        P("gx", "gy", None),
        P("gx", "gy", None),
        P("gx", "gy", None),
        P(None, "gx", "gy", None),
        P(None, "gx", "gy", None),
    )
    out_specs = (P("gx", "gy", None), P("gx", "gy", None))
    return jax.shard_map(body, mesh=mesh, in_specs=in_specs, out_specs=out_specs, check_vma=False)
```

```python
import functools
import math

import jax
import jax.numpy as jnp
import numpy as np
from jax import lax
from jax.experimental import pallas as pl
from jax.experimental.pallas import tpu as pltpu
from jax.sharding import PartitionSpec as P

STEPS = 2
NX, NY, NZ = 512, 256, 128
GX, GY = 64, 8
XL, YL = NX // GX, NY // GY
ROWS = XL * YL
time_step = 0.2

MESH = pl.DeviceIdType.MESH
F32, BF16 = jnp.float32, jnp.bfloat16


def real_form(matrix):
    return np.block([[matrix.real, matrix.imag], [-matrix.imag, matrix.real]])


def left_form(matrix):
    return np.block([[matrix.real, -matrix.imag], [matrix.imag, matrix.real]])


def dft(length, sign):
    k = np.arange(length)
    return np.exp(sign * 2j * math.pi * (np.outer(k, k) % length) / length)


def tables():
    z = np.arange(NZ)
    per = NZ // 2 // GY
    forward_z = np.zeros((NZ, NZ))
    weighted_z = np.zeros((NZ, NZ))
    back_z = np.zeros((NZ, NZ))
    weighted_back = np.zeros((NZ, NZ))
    norm = 1.0 / (NX * NY * NZ)
    for column in range(NZ // 2):
        real_row = (column // per) * 2 * per + column % per
        imag_row = real_row + per
        angle = 2 * math.pi * (column * z % NZ) / NZ
        cosine, sine = np.cos(angle), np.sin(angle)
        if column == 0:
            sign = 1.0 - 2.0 * (z % 2)
            forward_z[real_row], forward_z[imag_row] = 1.0, sign
            back_z[real_row], back_z[imag_row] = norm, norm * sign
        else:
            forward_z[real_row], forward_z[imag_row] = cosine, -sine
            back_z[real_row], back_z[imag_row] = 2 * norm * cosine, -2 * norm * sine
        weighted_z[real_row] = column * forward_z[real_row]
        weighted_z[imag_row] = column * forward_z[imag_row]
        weighted_back[real_row] = column * back_z[real_row]
        weighted_back[imag_row] = column * back_z[imag_row]

    device_y = np.kron(dft(GY, -1), np.eye(per))
    arrive = np.zeros((NZ, NZ))
    for source in range(GY):
        for part in range(2):
            for j in range(per):
                arrive[part * 64 + source * per + j, source * 2 * per + part * per + j] = 1.0
    left_y = left_form(device_y) @ arrive
    left_y_back = arrive.T @ left_form(device_y.conj())
    q1 = np.arange(64) // per
    yl = np.arange(ROWS) % YL
    turn_y = np.exp(-2j * math.pi * (np.outer(q1, yl) % NY) / NY)
    local_y = real_form(np.kron(np.eye(4), dft(YL, -1)))
    local_y_back = real_form(np.kron(np.eye(4), dft(YL, 1)))

    left_x = left_form(dft(GX, -1))
    left_x_back = left_form(dft(GX, 1))
    xl = np.arange(ROWS) // YL
    turn_x = np.exp(-2j * math.pi * (np.outer(np.arange(64), xl) % NX) / NX)
    local_x = []
    for a in range(2):
        small = np.diag(np.exp(-2j * math.pi * a * np.arange(4) / 8)) @ dft(4, -1)
        local_x.append(np.kron(small, np.eye(YL)))
    local_x_back = [real_form(m.conj().T) for m in local_x]
    local_x = [real_form(m) for m in local_x]

    def pair(stack):
        stack = np.stack(stack).astype(np.float32)
        high = stack.astype(BF16)
        low = (stack - high.astype(np.float32)).astype(BF16)
        return np.stack([high, low], axis=1)

    small = pair(
        [forward_z, weighted_z, left_y, left_y_back, left_x, left_x_back, back_z, weighted_back]
    )
    large = pair([local_y, local_y_back] + local_x + local_x_back)
    turns = np.stack([turn_y.real, turn_y.imag, turn_x.real, turn_x.imag]).astype(np.float32)
    return small, large, turns


def split(value):
    high = value.astype(BF16)
    return high, (value - high.astype(F32)).astype(BF16)


def product(left, right, dims):
    def one(a, b):
        return lax.dot_general(a, b, (dims, ((), ())), preferred_element_type=F32)

    return one(left[0], right[0]) + (one(left[0], right[1]) + one(left[1], right[0]))


NN = ((1,), (0,))
NT = ((1,), (1,))
TN = ((0,), (0,))


def matmul(left, right, dims=NN):
    left = left if isinstance(left, tuple) else split(left)
    right = right if isinstance(right, tuple) else split(right)
    return product(left, right, dims)


def turned(real, imag, cosine, sine, back):
    if back:
        return real * cosine + imag * sine, imag * cosine - real * sine
    return real * cosine - imag * sine, imag * cosine + real * sine


def lanes(value, half):
    return value[:, half * 128 : half * 128 + 128]


def z_forward(field, table):
    return matmul(table, field, NT)


def y_forward_left(arrived, left, cosine, sine):
    both = matmul(left, arrived)
    return turned(both[:64], both[64:], cosine, sine, False)


def halves_product(pairs, table):
    stacked = jnp.concatenate(
        [
            jnp.concatenate([lanes(re, h), lanes(im, h)], axis=1)
            for re, im in pairs
            for h in range(2)
        ],
        axis=0,
    )
    out = matmul(stacked, table)
    result = []
    for n in range(len(pairs)):
        rows = [out[(2 * n + h) * 64 : (2 * n + h) * 64 + 64] for h in range(2)]
        result.append(
            tuple(
                jnp.concatenate([r[:, part * 128 : part * 128 + 128] for r in rows], axis=1)
                for part in range(2)
            )
        )
    return result


def signed(positions, length):
    half = length // 2
    value = jnp.where(positions < half, positions, positions - length)
    return jnp.where(positions == half, 0, value).astype(F32)


def iota(axis):
    return lax.broadcasted_iota(jnp.int32, (64, 256), axis)


def wave_y_rows():
    return signed(iota(0) // 8 + 8 * (iota(1) % YL), NY)


def waves_here(gx, gy):
    lane = iota(1)
    k2 = lane // 128 + 2 * (lane % 128 // YL)
    wave_x = signed(iota(0) + 64 * k2, NX)
    wave_y = signed(gx // 8 + 8 * (lane % YL), NY)
    wave_z = (gy * 8 + gx % 8).astype(F32)
    size = wave_x * wave_x + wave_y * wave_y + wave_z * wave_z
    return wave_x, 1.0 / jnp.maximum(size, 1.0)


def x_stage(planes, left, left_back, local, local_back, cosine, sine, wave_x, inverse):
    stacked = jnp.concatenate(
        [
            jnp.concatenate([planes[2 * f][h], planes[2 * f + 1][h]], axis=0)
            for f in range(2)
            for h in range(2)
        ],
        axis=1,
    )
    out = matmul(left, stacked)
    fields = []
    for f in range(2):
        re, im = out[:64, f * 256 : f * 256 + 256], out[64:, f * 256 : f * 256 + 256]
        fields.append(turned(re, im, cosine, sine, False))
    spectra = [[], []]
    for a in range(2):
        rows = []
        for re, im in fields:
            if a == 0:
                re, im = lanes(re, 0) + lanes(re, 1), lanes(im, 0) + lanes(im, 1)
            else:
                re, im = lanes(re, 0) - lanes(re, 1), lanes(im, 0) - lanes(im, 1)
            rows.append(jnp.concatenate([re, im], axis=1))
        got = matmul(jnp.concatenate(rows, axis=0), local[a])
        wave = lanes(wave_x, a)
        scale = lanes(inverse, a)
        phi_re = (wave * got[:64, :128] + got[64:, :128]) * scale
        phi_im = (wave * got[:64, 128:] + got[64:, 128:]) * scale
        both = jnp.concatenate(
            [
                jnp.concatenate([wave * phi_re, wave * phi_im], axis=1),
                jnp.concatenate([phi_re, phi_im], axis=1),
            ],
            axis=0,
        )
        back = matmul(both, local_back[a])
        for f in range(2):
            spectra[a].append((back[f * 64 : f * 64 + 64, :128], back[f * 64 : f * 64 + 64, 128:]))
    stacked = []
    for f in range(2):
        zero, one = spectra[0][f], spectra[1][f]
        for h in range(2):
            if h == 0:
                re, im = zero[0] + one[0], zero[1] + one[1]
            else:
                re, im = zero[0] - one[0], zero[1] - one[1]
            re, im = turned(re, im, lanes(cosine, h), lanes(sine, h), True)
            stacked.append(jnp.concatenate([re, im], axis=0))
    out = matmul(left_back, jnp.concatenate(stacked, axis=1))
    result = []
    for f in range(2):
        for part in range(2):
            rows = out[part * 64 : part * 64 + 64]
            result.append(
                [rows[:, (2 * f + h) * 128 : (2 * f + h) * 128 + 128] for h in range(2)]
            )
    return result


def y_back_left(pair, left, cosine, sine):
    re, im = turned(pair[0], pair[1], cosine, sine, True)
    return matmul(left, jnp.concatenate([re, im], axis=0))


def z_back(arrived, table):
    return matmul(arrived, table, TN)


def kernel(
    velocity, stress, lame, shear, buoy, source_p, source_s, small, large, turns,
    image_p, image_s,
    v_0, v_1, v_2, s_0, s_1, rims, lame_v, shear_v, buoy_v, source_p_v, source_s_v,
    small_v, large_v, turns_v, moduli, y_send, y_recv, y_send_2, y_recv_2, corners,
    z_send, z_recv, x_send, x_recv, x_send_2, x_recv_2, z_send_2, z_recv_2,
    load_sem, halo_send, halo_recv, gy_send, gy_recv, gx_send, gx_recv,
):
    gx, gy = lax.axis_index("gx"), lax.axis_index("gy")

    barrier = pltpu.get_barrier_semaphore()

    def greet(device):
        pl.semaphore_signal(barrier, inc=1, device_id=device, device_id_type=MESH)

    def greet_x(k, carry):
        greet((lax.rem(gx + k, GX), gy))
        return carry

    def greet_y(k, carry):
        greet((gx, lax.rem(gy + k, GY)))
        return carry

    next_gx, prior_gx = lax.rem(gx + 1, GX), lax.rem(gx + GX - 1, GX)
    next_gy, prior_gy = lax.rem(gy + 1, GY), lax.rem(gy + GY - 1, GY)
    greet((next_gx, prior_gy))
    greet((prior_gx, next_gy))
    lax.fori_loop(1, GY, greet_y, 0)
    lax.fori_loop(1, GX, greet_x, 0)

    def interior(ref):
        return ref.at[:, pl.ds(YL, ROWS)]

    loads = [
        (lame, lame_v),
        (shear, shear_v),
        (velocity, interior(v_0)),
        (stress, interior(s_0)),
        (buoy, buoy_v),
        (small, small_v),
        (large, large_v),
        (turns, turns_v),
        (source_p, source_p_v),
        (source_s, source_s_v),
    ]
    loads = [pltpu.make_async_copy(a, b, load_sem.at[n]) for n, (a, b) in enumerate(loads)]
    for load in loads:
        load.start()

    def send(source, target, device, send_sem, recv_sem):
        copy = pltpu.make_async_remote_copy(
            src_ref=source,
            dst_ref=target,
            send_sem=send_sem,
            recv_sem=recv_sem,
            device_id=device,
            device_id_type=MESH,
        )
        copy.start()
        return copy

    first, last = pl.ds(YL, YL), pl.ds(ROWS, YL)
    below, above = pl.ds(0, YL), pl.ds(ROWS + YL, YL)
    top_rows = pl.ds(YL, XL, stride=YL)
    end_rows = pl.ds(2 * YL - 1, XL, stride=YL)
    every = pl.ds(0, 3)
    sent = []

    def exchange(turn, v, sending, receiving, more):
        plan = [
            (sending.at[0], receiving.at[0], (gx, next_gy)),
            (sending.at[1], receiving.at[1], (gx, prior_gy)),
            (sending.at[0, 1], corners.at[turn, 0], (prior_gx, next_gy)),
            (sending.at[1, 0], corners.at[turn, 1], (next_gx, prior_gy)),
            (v.at[every, last], v.at[every, below], (next_gx, gy)),
            (v.at[every, first], v.at[every, above], (prior_gx, gy)),
        ] + more
        copies = [
            send(source, target, device, halo_send.at[turn, n], halo_recv.at[turn, n])
            for n, (source, target, device) in enumerate(plan)
        ]
        sent.extend(copies)
        return copies

    def arrive(turn, copies, v, receiving, fields):
        for copy in copies:
            copy.wait_recv()
        nothing = jnp.zeros((YL, NZ), F32)

        @pl.when(gx == 0)
        def _():
            for n in range(3):
                v[n, below, :] = nothing
            if turn == 0:
                s_0[3, below, :] = nothing
                s_0[4, below, :] = nothing
                moduli[1, below, :] = nothing
            corners[turn, 1] = nothing[:XL]

        @pl.when(gx == GX - 1)
        def _():
            for n in range(3):
                v[n, above, :] = nothing
            if turn == 0:
                s_0[0, above, :] = nothing
                moduli[0, above, :] = nothing
                moduli[1, above, :] = nothing
            corners[turn, 0] = nothing[:XL]

        @pl.when(gy == 0)
        def _():
            for n in range(fields):
                receiving[0, n] = nothing[:XL]
            corners[turn, 0] = nothing[:XL]

        @pl.when(gy == GY - 1)
        def _():
            for n in range(fields):
                receiving[1, n] = nothing[:XL]
            corners[turn, 1] = nothing[:XL]

    def at_row(f, row):
        return lax.broadcasted_iota(jnp.int32, f.shape, 0) == row

    def at_lane(f, lane):
        return lax.broadcasted_iota(jnp.int32, f.shape, 1) == lane

    def next_z(f):
        return jnp.where(at_lane(f, NZ - 1), 0.0, pltpu.roll(f, NZ - 1, 1))

    def prior_z(f):
        return jnp.where(at_lane(f, 0), 0.0, pltpu.roll(f, 1, 1))

    def next_row(f, rim):
        return jnp.where(at_row(f, f.shape[0] - 1), rim, pltpu.roll(f, f.shape[0] - 1, 0))

    def prior_row(f, rim):
        return jnp.where(at_row(f, 0), rim, pltpu.roll(f, 1, 0))

    def plane_at(i):
        return i if isinstance(i, int) else pl.multiple_of(i, YL)

    def over_planes(plane):
        plane(0, False, True)

        def middle(i, carry):
            plane(i, True, True)
            return carry

        lax.fori_loop(1, XL - 1, middle, 0)
        plane(XL - 1, True, False)

    def stress_inside(v, s_in, s_out):
        def plane(i, has_before, has_after):
            here = pl.ds(plane_at((i + 1) * YL), YL)
            before = pl.ds(plane_at(i * YL), YL)
            after = pl.ds(plane_at((i + 2) * YL), YL)
            v_x, v_y, v_z = v[0, here, :], v[1, here, :], v[2, here, :]
            lam, mu = moduli[0, here, :], moduli[1, here, :]
            e_x = v_x - v[0, before, :] if has_before else v_x
            e_y = v_y - prior_row(v_y, 0.0)
            e_z = v_z - prior_z(v_z)
            x_y = v[1, after, :] - v_y if has_after else -v_y
            x_z = v[2, after, :] - v_z if has_after else -v_z
            volume = lam * (e_x + e_y + e_z)
            twice = 2.0 * mu
            s_out[0, here, :] = s_in[0, here, :] + (volume + twice * e_x)
            s_out[1, here, :] = s_in[1, here, :] + (volume + twice * e_y)
            s_out[2, here, :] = s_in[2, here, :] + (volume + twice * e_z)
            s_out[3, here, :] = s_in[3, here, :] + mu * ((next_row(v_x, 0.0) - v_x) + x_y)
            s_out[4, here, :] = s_in[4, here, :] + mu * ((next_z(v_x) - v_x) + x_z)
            s_out[5, here, :] = s_in[5, here, :] + mu * (
                (next_z(v_y) - v_y) + (next_row(v_z, 0.0) - v_z)
            )

        over_planes(plane)

    def stress_rims(v, s_in, s_out, received, turn):
        prior_side = [received[0, n] for n in range(3)]
        next_side = [received[1, n] for n in range(3)]
        corner_y = corners[turn, 0, pl.ds(0, 1), :]
        corner_x = corners[turn, 1, pl.ds(XL - 1, 1), :]

        gone = v[0, below, :]
        lam, mu = moduli[0, first, :], moduli[1, first, :]
        s_out[0, first, :] -= (lam + 2.0 * mu) * gone
        s_out[1, first, :] -= lam * gone
        s_out[2, first, :] -= lam * gone
        mu = moduli[1, last, :]
        s_out[3, last, :] += mu * v[1, above, :]
        s_out[4, last, :] += mu * v[2, above, :]

        gone = prior_side[1]
        lam, mu = moduli[0, top_rows, :], moduli[1, top_rows, :]
        s_out[0, top_rows, :] -= lam * gone
        s_out[1, top_rows, :] -= (lam + 2.0 * mu) * gone
        s_out[2, top_rows, :] -= lam * gone
        mu = moduli[1, end_rows, :]
        s_out[3, end_rows, :] += mu * next_side[0]
        s_out[5, end_rows, :] += mu * next_side[2]

        v_x, v_y, v_z = v[0, above, :], v[1, above, :], v[2, above, :]
        lam, mu = moduli[0, above, :], moduli[1, above, :]
        e_x = v_x - v[0, last, :]
        e_y = v_y - prior_row(v_y, corner_y)
        e_z = v_z - prior_z(v_z)
        s_out[0, above, :] = s_in[0, above, :] + (lam * (e_x + e_y + e_z) + 2.0 * mu * e_x)

        v_x, v_y, v_z = v[0, below, :], v[1, below, :], v[2, below, :]
        mu = moduli[1, below, :]
        s_out[3, below, :] = s_in[3, below, :] + mu * (
            (next_row(v_x, corner_x) - v_x) + (v[1, first, :] - v_y)
        )
        s_out[4, below, :] = s_in[4, below, :] + mu * (
            (next_z(v_x) - v_x) + (v[2, first, :] - v_z)
        )

        v_x, v_y, v_z = next_side
        lam, mu = y_recv[1, 4], y_recv[1, 5]
        e_x = v_x - prior_row(v_x, corner_x)
        e_y = v_y - v[1, end_rows, :]
        e_z = v_z - prior_z(v_z)
        old = y_recv[1, 3] if turn == 0 else rims[0]
        rims[0] = old + (lam * (e_x + e_y + e_z) + 2.0 * mu * e_y)

        v_x, v_y, v_z = prior_side
        mu = y_recv[0, 5]
        old = y_recv[0, 3] if turn == 0 else rims[1]
        rims[1] = old + mu * ((v[0, top_rows, :] - v_x) + (next_row(v_y, corner_y) - v_y))
        old = y_recv[0, 4] if turn == 0 else rims[2]
        rims[2] = old + mu * ((next_z(v_y) - v_y) + (v[2, top_rows, :] - v_z))

    def velocity_update(v_in, s, v_out):
        def plane(i, carry):
            here = pl.ds(pl.multiple_of((i + 1) * YL, YL), YL)
            before = pl.ds(pl.multiple_of(i * YL, YL), YL)
            after = pl.ds(pl.multiple_of((i + 2) * YL, YL), YL)
            inner = pl.ds(pl.multiple_of(i * YL, YL), YL)

            def rim(n):
                return rims[n, pl.ds(i, 1), :]

            b = buoy_v[inner, :].astype(F32) * time_step
            xx, yy, zz = s[0, here, :], s[1, here, :], s[2, here, :]
            xy, xz, yz = s[3, here, :], s[4, here, :], s[5, here, :]
            v_out[0, here, :] = v_in[0, here, :] + b * (
                (s[0, after, :] - xx) + (xy - prior_row(xy, rim(1))) + (xz - prior_z(xz))
            )
            v_out[1, here, :] = v_in[1, here, :] + b * (
                (xy - s[3, before, :]) + (next_row(yy, rim(0)) - yy) + (yz - prior_z(yz))
            )
            v_out[2, here, :] = v_in[2, here, :] + b * (
                (xz - s[4, before, :]) + (yz - prior_row(yz, rim(2))) + (next_z(zz) - zz)
            )
            return carry

        lax.fori_loop(0, XL, plane, 0)

    for load in loads[:2]:
        load.wait()
    moduli[0, pl.ds(YL, ROWS), :] = lame_v[...].astype(F32) * time_step
    moduli[1, pl.ds(YL, ROWS), :] = shear_v[...].astype(F32) * time_step
    for load in loads[2:4]:
        load.wait()
    for side, rows in enumerate([end_rows, top_rows]):
        for n in range(3):
            y_send[side, n] = v_0[n, rows, :]
        y_send[side, 5] = moduli[1, rows, :]
    y_send[0, 3] = s_0[3, end_rows, :]
    y_send[0, 4] = s_0[5, end_rows, :]
    y_send[1, 3] = s_0[1, top_rows, :]
    y_send[1, 4] = moduli[0, top_rows, :]
    pl.semaphore_wait(barrier, GX + GY)

    shears, both, only, one = pl.ds(3, 2), pl.ds(0, 2), pl.ds(0, 1), pl.ds(1, 1)
    copies = exchange(
        0,
        v_0,
        y_send,
        y_recv,
        [
            (s_0.at[shears, last], s_0.at[shears, below], (next_gx, gy)),
            (s_0.at[only, first], s_0.at[only, above], (prior_gx, gy)),
            (moduli.at[one, last], moduli.at[one, below], (next_gx, gy)),
            (moduli.at[both, first], moduli.at[both, above], (prior_gx, gy)),
        ],
    )
    stress_inside(v_0, s_0, s_1)
    arrive(0, copies, v_0, y_recv, 6)
    stress_rims(v_0, s_0, s_1, y_recv, 0)
    loads[4].wait()
    velocity_update(v_0, s_1, v_1)
    for side, rows in enumerate([end_rows, top_rows]):
        for n in range(3):
            y_send_2[side, n] = v_1[n, rows, :]
    copies = exchange(1, v_1, y_send_2, y_recv_2, [])
    stress_inside(v_1, s_1, s_1)
    arrive(1, copies, v_1, y_recv_2, 3)
    stress_rims(v_1, s_1, s_1, y_recv_2, 1)
    velocity_update(v_1, s_1, v_2)

    for load in loads[5:8]:
        load.wait()

    def narrow(n):
        return small_v[n, 0], small_v[n, 1]

    def wide(n):
        return large_v[n, 0], large_v[n, 1]

    def all_to_all_gy(field, sent, received, turn):
        mine = pl.ds(pl.multiple_of(gy * 16, 16), 16)

        def one(k, carry):
            to = lax.rem(gy + k, GY)
            send(
                sent.at[field, pl.ds(pl.multiple_of(to * 16, 16), 16)],
                received.at[field, mine],
                (gx, to),
                gy_send.at[turn, field],
                gy_recv.at[turn, field],
            )
            return carry

        lax.fori_loop(1, GY, one, 0)
        received[field, mine, :] = sent[field, mine, :]

    def wait_gy(field, received, sems, turn):
        part = received.at[field, pl.ds(0, 16 * (GY - 1))]
        pltpu.make_async_copy(part, part, sems.at[turn, field]).wait()

    def all_to_all_gx(sent, received, turn):
        mine = pl.ds(pl.multiple_of(gx * 8, 8), 8)

        def one(k, carry):
            to = lax.rem(gx + k, GX)
            send(
                sent.at[pl.ds(pl.multiple_of(to * 8, 8), 8)],
                received.at[mine],
                (to, gy),
                gx_send.at[turn],
                gx_recv.at[turn],
            )
            return carry

        lax.fori_loop(1, GX, one, 0)
        received[mine, :] = sent[mine, :]

    def wait_gx(received, sems, turn):
        part = received.at[pl.ds(0, 8 * (GX - 1))]
        pltpu.make_async_copy(part, part, sems.at[turn]).wait()

    turn_y = turns_v[0], turns_v[1]
    turn_x = turns_v[2], turns_v[3]

    for field in range(3):
        table = narrow(1 if field == 2 else 0)
        z_send[field] = z_forward(v_2[field, pl.ds(YL, ROWS), :], table)
        all_to_all_gy(field, z_send, z_recv, 0)

    pairs = []
    for field in range(3):
        wait_gy(field, z_recv, gy_recv, 0)
        pairs.append(y_forward_left(z_recv[field], narrow(2), *turn_y))
    pairs = halves_product(pairs, wide(0))
    wave_y = wave_y_rows()
    joined = [wave_y * pairs[1][part] + pairs[2][part] for part in range(2)]
    for p, value in enumerate([pairs[0][0], pairs[0][1]] + joined):
        for h in range(2):
            x_send[pl.ds(2 * p + h, 64, stride=8), :] = lanes(value, h)
    all_to_all_gx(x_send, x_recv, 0)

    wave_x, inverse = waves_here(gx, gy)
    wait_gx(x_recv, gx_recv, 0)
    planes = [[x_recv[pl.ds(2 * p + h, 64, stride=8), :] for h in range(2)] for p in range(4)]
    planes = x_stage(
        planes,
        narrow(4),
        narrow(5),
        [wide(2), wide(3)],
        [wide(4), wide(5)],
        *turn_x,
        wave_x,
        inverse,
    )
    for p in range(4):
        for h in range(2):
            x_send_2[pl.ds(2 * p + h, 64, stride=8), :] = planes[p][h]
    all_to_all_gx(x_send_2, x_recv_2, 1)

    wait_gx(x_recv_2, gx_recv, 1)
    planes = [
        jnp.concatenate([x_recv_2[pl.ds(2 * p + h, 64, stride=8), :] for h in range(2)], axis=1)
        for p in range(4)
    ]
    pairs = [
        (planes[0], planes[1]),
        (wave_y * planes[2], wave_y * planes[3]),
        (planes[2], planes[3]),
    ]
    pairs = halves_product(pairs, wide(1))
    for field in range(3):
        z_send_2[field] = y_back_left(pairs[field], narrow(3), *turn_y)
        all_to_all_gy(field, z_send_2, z_recv_2, 1)

    for load in loads[8:]:
        load.wait()
    total_p = jnp.zeros((ROWS, NZ), F32)
    total_s = jnp.zeros((ROWS, NZ), F32)
    for field in range(3):
        wait_gy(field, z_recv_2, gy_recv, 1)
        p_field = z_back(z_recv_2[field], narrow(7 if field == 2 else 6))
        s_field = v_2[field, pl.ds(YL, ROWS), :] - p_field
        total_p += source_p_v[field].astype(F32) * p_field
        total_s += source_s_v[field].astype(F32) * s_field
    image_p[...] = total_p
    image_s[...] = total_s

    for copy in sent:
        copy.wait_send()
    for field in range(3):
        wait_gy(field, z_send, gy_send, 0)
        wait_gy(field, z_send_2, gy_send, 1)
    wait_gx(x_send, gx_send, 0)
    wait_gx(x_send_2, gx_send, 1)


def shards(small, large, turns, velocity, stress, lame, shear, buoy, source_p, source_s):
    in_place = pl.BlockSpec(memory_space=pltpu.HBM)
    padded = (XL + 2) * YL
    dma = pltpu.SemaphoreType.DMA
    scratch = [
        *[pltpu.VMEM((3, padded, NZ), F32)] * 3,
        *[pltpu.VMEM((6, padded, NZ), F32)] * 2,
        pltpu.VMEM((3, XL, NZ), F32),
        *[pltpu.VMEM((ROWS, NZ), BF16)] * 3,
        *[pltpu.VMEM((3, ROWS, NZ), BF16)] * 2,
        pltpu.VMEM(small.shape, BF16),
        pltpu.VMEM(large.shape, BF16),
        pltpu.VMEM(turns.shape, F32),
        pltpu.VMEM((2, padded, NZ), F32),
        *[pltpu.VMEM((2, 6, XL, NZ), F32)] * 2,
        *[pltpu.VMEM((2, 3, XL, NZ), F32)] * 2,
        pltpu.VMEM((2, 2, XL, NZ), F32),
        *[pltpu.VMEM((3, NZ, ROWS), F32)] * 2,
        *[pltpu.VMEM((8 * GX, NZ), F32)] * 4,
        *[pltpu.VMEM((3, NZ, ROWS), F32)] * 2,
        dma((10,)),
        dma((2, 10)),
        dma((2, 10)),
        dma((2, 3)),
        dma((2, 3)),
        dma((2,)),
        dma((2,)),
    ]
    out = jax.ShapeDtypeStruct((ROWS, NZ), F32)
    outs = pl.pallas_call(
        kernel,
        out_shape=(out, out),
        in_specs=[in_place] * 10,
        out_specs=(pl.BlockSpec(memory_space=pltpu.VMEM),) * 2,
        scratch_shapes=scratch,
        compiler_params=pltpu.CompilerParams(
            collective_id=0, has_side_effects=True, vmem_limit_bytes=60 * 2**20
        ),
    )(
        velocity.reshape(3, ROWS, NZ),
        stress.reshape(6, ROWS, NZ),
        lame.reshape(ROWS, NZ),
        shear.reshape(ROWS, NZ),
        buoy.reshape(ROWS, NZ),
        source_p.reshape(3, ROWS, NZ),
        source_s.reshape(3, ROWS, NZ),
        small,
        large,
        turns,
    )
    return tuple(o.reshape(XL, YL, NZ) for o in outs)


def solution(mesh):
    small, large, turns = tables()

    def body(*blocks):
        return shards(jnp.asarray(small), jnp.asarray(large), jnp.asarray(turns), *blocks)

    in_specs = (
        P(None, "gx", "gy", None),
        P(None, "gx", "gy", None),
        P("gx", "gy", None),
        P("gx", "gy", None),
        P("gx", "gy", None),
        P(None, "gx", "gy", None),
        P(None, "gx", "gy", None),
    )
    out_specs = (P("gx", "gy", None), P("gx", "gy", None))
    return jax.shard_map(body, mesh=mesh, in_specs=in_specs, out_specs=out_specs, check_vma=False)
```

```python
import functools
import math

import jax
import jax.numpy as jnp
import numpy as np
from jax import lax
from jax.experimental import pallas as pl
from jax.experimental.pallas import tpu as pltpu
from jax.sharding import PartitionSpec as P

STEPS = 2
NX, NY, NZ = 512, 256, 128
GX, GY = 64, 8
XL, YL = NX // GX, NY // GY
ROWS = XL * YL
time_step = 0.2

MESH = pl.DeviceIdType.MESH
F32, BF16 = jnp.float32, jnp.bfloat16


def real_form(matrix):
    return np.block([[matrix.real, matrix.imag], [-matrix.imag, matrix.real]])


def left_form(matrix):
    return np.block([[matrix.real, -matrix.imag], [matrix.imag, matrix.real]])


def dft(length, sign):
    k = np.arange(length)
    return np.exp(sign * 2j * math.pi * (np.outer(k, k) % length) / length)


def tables():
    z = np.arange(NZ)
    forward_z = np.zeros((NZ, NZ))
    weighted_z = np.zeros((NZ, NZ))
    back_z = np.zeros((NZ, NZ))
    weighted_back = np.zeros((NZ, NZ))
    norm = 1.0 / (NX * NY * NZ)
    for column in range(NZ // 2):
        real_row, imag_row = column, NZ // 2 + column
        angle = 2 * math.pi * (column * z % NZ) / NZ
        cosine, sine = np.cos(angle), np.sin(angle)
        if column == 0:
            sign = 1.0 - 2.0 * (z % 2)
            forward_z[real_row], forward_z[imag_row] = 1.0, sign
            back_z[real_row], back_z[imag_row] = norm, norm * sign
        else:
            forward_z[real_row], forward_z[imag_row] = cosine, -sine
            back_z[real_row], back_z[imag_row] = 2 * norm * cosine, -2 * norm * sine
        weighted_z[real_row] = column * forward_z[real_row]
        weighted_z[imag_row] = column * forward_z[imag_row]
        weighted_back[real_row] = column * back_z[real_row]
        weighted_back[imag_row] = column * back_z[imag_row]

    per = NX // 64
    left_y = left_form(np.kron(dft(GY, -1), np.eye(per)))
    left_y_back = left_form(np.kron(dft(GY, 1), np.eye(per)))
    q1 = np.arange(64) // per
    yl = np.arange(ROWS) % YL
    turn_y = np.exp(-2j * math.pi * (np.outer(q1, yl) % NY) / NY)
    local_y = real_form(np.kron(np.eye(4), dft(YL, -1)))
    local_y_back = real_form(np.kron(np.eye(4), dft(YL, 1)))

    left_x = left_form(dft(GX, -1))
    left_x_back = left_form(dft(GX, 1))
    xl = np.arange(ROWS) // YL
    turn_x = np.exp(-2j * math.pi * (np.outer(np.arange(64), xl) % NX) / NX)
    local_x = []
    for a in range(2):
        small = np.diag(np.exp(-2j * math.pi * a * np.arange(4) / 8)) @ dft(4, -1)
        local_x.append(np.kron(small, np.eye(YL)))
    local_x_back = [real_form(m.conj().T) for m in local_x]
    local_x = [real_form(m) for m in local_x]

    def pair(stack):
        stack = np.stack(stack).astype(np.float32)
        high = stack.astype(BF16)
        low = (stack - high.astype(np.float32)).astype(BF16)
        return np.stack([high, low], axis=1)

    small = pair(
        [forward_z, weighted_z, left_y, left_y_back, left_x, left_x_back, back_z, weighted_back]
    )
    large = pair([local_y, local_y_back] + local_x + local_x_back)
    turns = np.stack([turn_y.real, turn_y.imag, turn_x.real, turn_x.imag]).astype(np.float32)
    return small, large, turns


def split(value):
    high = value.astype(BF16)
    return high, (value - high.astype(F32)).astype(BF16)


def product(left, right, dims):
    def one(a, b):
        return lax.dot_general(a, b, (dims, ((), ())), preferred_element_type=F32)

    return one(left[0], right[0]) + (one(left[0], right[1]) + one(left[1], right[0]))


NN = ((1,), (0,))
NT = ((1,), (1,))
TN = ((0,), (0,))


def matmul(left, right, dims=NN):
    left = left if isinstance(left, tuple) else split(left)
    right = right if isinstance(right, tuple) else split(right)
    return product(left, right, dims)


def turned(real, imag, cosine, sine, back):
    if back:
        return real * cosine + imag * sine, imag * cosine - real * sine
    return real * cosine - imag * sine, imag * cosine + real * sine


def lanes(value, half):
    return value[:, half * 128 : half * 128 + 128]


def z_forward(field, table):
    return matmul(table, field, NT)


def y_forward_left(arrived, left, cosine, sine):
    both = matmul(left, arrived)
    return turned(both[:64], both[64:], cosine, sine, False)


def halves_product(pairs, table):
    stacked = jnp.concatenate(
        [
            jnp.concatenate([lanes(re, h), lanes(im, h)], axis=1)
            for re, im in pairs
            for h in range(2)
        ],
        axis=0,
    )
    out = matmul(stacked, table)
    result = []
    for n in range(len(pairs)):
        rows = [out[(2 * n + h) * 64 : (2 * n + h) * 64 + 64] for h in range(2)]
        result.append(
            tuple(
                jnp.concatenate([r[:, part * 128 : part * 128 + 128] for r in rows], axis=1)
                for part in range(2)
            )
        )
    return result


def signed(positions, length):
    half = length // 2
    value = jnp.where(positions < half, positions, positions - length)
    return jnp.where(positions == half, 0, value).astype(F32)


def iota(axis):
    return lax.broadcasted_iota(jnp.int32, (64, 256), axis)


def wave_x_of(first, rows):
    lane = iota(1)
    return signed(first + rows + 64 * (lane // 128 + 2 * (lane % 128 // YL)), NX)


def waves_here(place, column):
    wave_x = wave_x_of(place * 8, iota(0) % 8)
    wave_y = signed(iota(0) // 8 + 8 * (iota(1) % YL), NY)
    wave_z = column.astype(F32)
    size = wave_x * wave_x + wave_y * wave_y + wave_z * wave_z
    return wave_y, 1.0 / jnp.maximum(size, 1.0)


def rows_of(value, n):
    return value[n * 64 : n * 64 + 64]


def x_forward(fields, left, local, cosine, sine):
    stacked = [
        jnp.concatenate([planes[h], planes[2 + h]], axis=0) for planes in fields for h in range(2)
    ]
    out = matmul(left, jnp.concatenate(stacked, axis=1))
    even, odd = [], []
    for n in range(len(fields)):
        block = out[:, n * 256 : n * 256 + 256]
        pair = turned(block[:64], block[64:], cosine, sine, False)
        even.append(jnp.concatenate([lanes(v, 0) + lanes(v, 1) for v in pair], axis=1))
        odd.append(jnp.concatenate([lanes(v, 0) - lanes(v, 1) for v in pair], axis=1))
    both = [matmul(jnp.concatenate(v, axis=0), t) for v, t in zip((even, odd), local)]
    return [
        [
            jnp.concatenate([lanes(rows_of(v, n), part) for v in both], axis=1)
            for part in range(2)
        ]
        for n in range(len(fields))
    ]


def x_backward(pairs, left, local, cosine, sine):
    zero, one = [
        matmul(
            jnp.concatenate(
                [jnp.concatenate([lanes(v, a) for v in pair], axis=1) for pair in pairs], axis=0
            ),
            local[a],
        )
        for a in range(2)
    ]
    stacked = []
    for n in range(len(pairs)):
        for h in range(2):
            even, odd = rows_of(zero, n), rows_of(one, n)
            both = even + odd if h == 0 else even - odd
            re, im = turned(
                lanes(both, 0), lanes(both, 1), lanes(cosine, h), lanes(sine, h), True
            )
            stacked.append(jnp.concatenate([re, im], axis=0))
    out = matmul(left, jnp.concatenate(stacked, axis=1))
    return [
        [lanes(rows_of(out, part), 2 * n + h) for part in range(2) for h in range(2)]
        for n in range(len(pairs))
    ]


def y_back_left(pair, left, cosine, sine):
    re, im = turned(pair[0], pair[1], cosine, sine, True)
    return matmul(left, jnp.concatenate([re, im], axis=0))


def z_back(arrived, table):
    return matmul(arrived, table, TN)


def kernel(
    velocity, stress, lame, shear, buoy, source_p, source_s, small, large, turns,
    image_p, image_s,
    v_0, v_1, v_2, s_0, s_1, rims, lame_v, shear_v, buoy_v, source_p_v, source_s_v,
    small_v, large_v, turns_v, moduli, y_send, y_recv, y_send_2, y_recv_2, corners,
    waves, z_two, z_one, x_recv, x_send, x_recv_2, x_send_2, z_two_back, z_one_back,
    x_back, x_home, load_sem, halo_send, halo_recv,
    two_send, one_send, plane_recv, ring_send, ring_recv,
):
    gx, gy = lax.axis_index("gx"), lax.axis_index("gy")

    barrier = pltpu.get_barrier_semaphore()

    def greet(device):
        pl.semaphore_signal(barrier, inc=1, device_id=device, device_id_type=MESH)

    core, place = gx % 2, gy // 2 * 2 + gx % 2
    column = gy % 2 * 32 + gx // 2

    def in_plane(k, its_core):
        other = (column + k) % 64
        return other, (other % 32 * 2 + its_core, gy // 2 * 2 + other // 32)

    def in_ring(k):
        other = (place + k) % 8
        return other, (gx // 2 * 2 + other % 2, other // 2 * 2 + gy % 2)

    def greet_plane(k, carry):
        greet(in_plane(k, 0)[1])
        greet(in_plane(k, 1)[1])
        return carry

    def greet_ring(k, carry):
        greet(in_ring(k)[1])
        return carry

    next_gx, prior_gx = lax.rem(gx + 1, GX), lax.rem(gx + GX - 1, GX)
    next_gy, prior_gy = lax.rem(gy + 1, GY), lax.rem(gy + GY - 1, GY)
    def interior(ref):
        return ref.at[:, pl.ds(YL, ROWS)]

    loads = [
        (lame, lame_v),
        (shear, shear_v),
        (velocity, interior(v_0)),
        (stress, interior(s_0)),
        (buoy, buoy_v),
        (small, small_v),
        (large, large_v),
        (turns, turns_v),
        (source_p, source_p_v),
        (source_s, source_s_v),
    ]
    loads = [pltpu.make_async_copy(a, b, load_sem.at[n]) for n, (a, b) in enumerate(loads)]
    for load in loads:
        load.start()
    lax.fori_loop(1, 64, greet_plane, 0)
    lax.fori_loop(1, 8, greet_ring, 0)
    greet((gx, next_gy))
    greet((gx, prior_gy))
    greet((next_gx, prior_gy))
    greet((prior_gx, next_gy))

    def send(source, target, device, send_sem, recv_sem):
        copy = pltpu.make_async_remote_copy(
            src_ref=source,
            dst_ref=target,
            send_sem=send_sem,
            recv_sem=recv_sem,
            device_id=device,
            device_id_type=MESH,
        )
        copy.start()
        return copy

    first, last = pl.ds(YL, YL), pl.ds(ROWS, YL)
    below, above = pl.ds(0, YL), pl.ds(ROWS + YL, YL)
    top_rows = pl.ds(YL, XL, stride=YL)
    end_rows = pl.ds(2 * YL - 1, XL, stride=YL)
    every = pl.ds(0, 3)
    sent = []

    def exchange(turn, v, sending, receiving, more):
        plan = [
            (sending.at[0], receiving.at[0], (gx, next_gy)),
            (sending.at[1], receiving.at[1], (gx, prior_gy)),
            (sending.at[0, 1], corners.at[turn, 0], (prior_gx, next_gy)),
            (sending.at[1, 0], corners.at[turn, 1], (next_gx, prior_gy)),
            (v.at[every, last], v.at[every, below], (next_gx, gy)),
            (v.at[every, first], v.at[every, above], (prior_gx, gy)),
        ] + more
        copies = [
            send(source, target, device, halo_send.at[turn, n], halo_recv.at[turn, n])
            for n, (source, target, device) in enumerate(plan)
        ]
        sent.extend(copies)
        return copies

    def arrive(turn, copies, v, receiving, fields):
        for copy in copies:
            copy.wait_recv()
        nothing = jnp.zeros((YL, NZ), F32)

        @pl.when(gx == 0)
        def _():
            for n in range(3):
                v[n, below, :] = nothing
            if turn == 0:
                s_0[3, below, :] = nothing
                s_0[4, below, :] = nothing
                moduli[1, below, :] = nothing
            corners[turn, 1] = nothing[:XL]

        @pl.when(gx == GX - 1)
        def _():
            for n in range(3):
                v[n, above, :] = nothing
            if turn == 0:
                s_0[0, above, :] = nothing
                moduli[0, above, :] = nothing
                moduli[1, above, :] = nothing
            corners[turn, 0] = nothing[:XL]

        @pl.when(gy == 0)
        def _():
            for n in range(fields):
                receiving[0, n] = nothing[:XL]
            corners[turn, 0] = nothing[:XL]

        @pl.when(gy == GY - 1)
        def _():
            for n in range(fields):
                receiving[1, n] = nothing[:XL]
            corners[turn, 1] = nothing[:XL]

    def at_row(f, row):
        return lax.broadcasted_iota(jnp.int32, f.shape, 0) == row

    def at_lane(f, lane):
        return lax.broadcasted_iota(jnp.int32, f.shape, 1) == lane

    def next_z(f):
        return jnp.where(at_lane(f, NZ - 1), 0.0, pltpu.roll(f, NZ - 1, 1))

    def prior_z(f):
        return jnp.where(at_lane(f, 0), 0.0, pltpu.roll(f, 1, 1))

    def next_row(f, rim):
        return jnp.where(at_row(f, f.shape[0] - 1), rim, pltpu.roll(f, f.shape[0] - 1, 0))

    def prior_row(f, rim):
        return jnp.where(at_row(f, 0), rim, pltpu.roll(f, 1, 0))

    def plane_at(i):
        return i if isinstance(i, int) else pl.multiple_of(i, YL)

    def over_planes(plane):
        plane(0, False, True)

        def middle(i, carry):
            plane(i, True, True)
            return carry

        lax.fori_loop(1, XL - 1, middle, 0)
        plane(XL - 1, True, False)

    def stress_inside(v, s_in, s_out):
        def plane(i, has_before, has_after):
            here = pl.ds(plane_at((i + 1) * YL), YL)
            before = pl.ds(plane_at(i * YL), YL)
            after = pl.ds(plane_at((i + 2) * YL), YL)
            v_x, v_y, v_z = v[0, here, :], v[1, here, :], v[2, here, :]
            lam, mu = moduli[0, here, :], moduli[1, here, :]
            e_x = v_x - v[0, before, :] if has_before else v_x
            e_y = v_y - prior_row(v_y, 0.0)
            e_z = v_z - prior_z(v_z)
            x_y = v[1, after, :] - v_y if has_after else -v_y
            x_z = v[2, after, :] - v_z if has_after else -v_z
            volume = lam * (e_x + e_y + e_z)
            twice = 2.0 * mu
            s_out[0, here, :] = s_in[0, here, :] + (volume + twice * e_x)
            s_out[1, here, :] = s_in[1, here, :] + (volume + twice * e_y)
            s_out[2, here, :] = s_in[2, here, :] + (volume + twice * e_z)
            s_out[3, here, :] = s_in[3, here, :] + mu * ((next_row(v_x, 0.0) - v_x) + x_y)
            s_out[4, here, :] = s_in[4, here, :] + mu * ((next_z(v_x) - v_x) + x_z)
            s_out[5, here, :] = s_in[5, here, :] + mu * (
                (next_z(v_y) - v_y) + (next_row(v_z, 0.0) - v_z)
            )

        over_planes(plane)

    def stress_rims(v, s_in, s_out, received, turn):
        prior_side = [received[0, n] for n in range(3)]
        next_side = [received[1, n] for n in range(3)]
        corner_y = corners[turn, 0, pl.ds(0, 1), :]
        corner_x = corners[turn, 1, pl.ds(XL - 1, 1), :]

        gone = v[0, below, :]
        lam, mu = moduli[0, first, :], moduli[1, first, :]
        s_out[0, first, :] -= (lam + 2.0 * mu) * gone
        s_out[1, first, :] -= lam * gone
        s_out[2, first, :] -= lam * gone
        mu = moduli[1, last, :]
        s_out[3, last, :] += mu * v[1, above, :]
        s_out[4, last, :] += mu * v[2, above, :]

        gone = prior_side[1]
        lam, mu = moduli[0, top_rows, :], moduli[1, top_rows, :]
        s_out[0, top_rows, :] -= lam * gone
        s_out[1, top_rows, :] -= (lam + 2.0 * mu) * gone
        s_out[2, top_rows, :] -= lam * gone
        mu = moduli[1, end_rows, :]
        s_out[3, end_rows, :] += mu * next_side[0]
        s_out[5, end_rows, :] += mu * next_side[2]

        v_x, v_y, v_z = v[0, above, :], v[1, above, :], v[2, above, :]
        lam, mu = moduli[0, above, :], moduli[1, above, :]
        e_x = v_x - v[0, last, :]
        e_y = v_y - prior_row(v_y, corner_y)
        e_z = v_z - prior_z(v_z)
        s_out[0, above, :] = s_in[0, above, :] + (lam * (e_x + e_y + e_z) + 2.0 * mu * e_x)

        v_x, v_y, v_z = v[0, below, :], v[1, below, :], v[2, below, :]
        mu = moduli[1, below, :]
        s_out[3, below, :] = s_in[3, below, :] + mu * (
            (next_row(v_x, corner_x) - v_x) + (v[1, first, :] - v_y)
        )
        s_out[4, below, :] = s_in[4, below, :] + mu * (
            (next_z(v_x) - v_x) + (v[2, first, :] - v_z)
        )

        v_x, v_y, v_z = next_side
        lam, mu = y_recv[1, 4], y_recv[1, 5]
        e_x = v_x - prior_row(v_x, corner_x)
        e_y = v_y - v[1, end_rows, :]
        e_z = v_z - prior_z(v_z)
        old = y_recv[1, 3] if turn == 0 else rims[0]
        rims[0] = old + (lam * (e_x + e_y + e_z) + 2.0 * mu * e_y)

        v_x, v_y, v_z = prior_side
        mu = y_recv[0, 5]
        old = y_recv[0, 3] if turn == 0 else rims[1]
        rims[1] = old + mu * ((v[0, top_rows, :] - v_x) + (next_row(v_y, corner_y) - v_y))
        old = y_recv[0, 4] if turn == 0 else rims[2]
        rims[2] = old + mu * ((next_z(v_y) - v_y) + (v[2, top_rows, :] - v_z))

    def velocity_update(v_in, s, v_out):
        def plane(i, carry):
            here = pl.ds(pl.multiple_of((i + 1) * YL, YL), YL)
            before = pl.ds(pl.multiple_of(i * YL, YL), YL)
            after = pl.ds(pl.multiple_of((i + 2) * YL, YL), YL)
            inner = pl.ds(pl.multiple_of(i * YL, YL), YL)

            def rim(n):
                return rims[n, pl.ds(i, 1), :]

            b = buoy_v[inner, :].astype(F32) * time_step
            xx, yy, zz = s[0, here, :], s[1, here, :], s[2, here, :]
            xy, xz, yz = s[3, here, :], s[4, here, :], s[5, here, :]
            v_out[0, here, :] = v_in[0, here, :] + b * (
                (s[0, after, :] - xx) + (xy - prior_row(xy, rim(1))) + (xz - prior_z(xz))
            )
            v_out[1, here, :] = v_in[1, here, :] + b * (
                (xy - s[3, before, :]) + (next_row(yy, rim(0)) - yy) + (yz - prior_z(yz))
            )
            v_out[2, here, :] = v_in[2, here, :] + b * (
                (xz - s[4, before, :]) + (yz - prior_row(yz, rim(2))) + (next_z(zz) - zz)
            )
            return carry

        lax.fori_loop(0, XL, plane, 0)

    wave_x = wave_x_of(0, iota(0))
    waves[0] = jnp.where(core == 0, wave_x, 1.0)
    waves[1], waves[2] = waves_here(place, column)

    @pl.when(core == 1)
    def _():
        x_recv[:, 1] = jnp.zeros((128, 4, 128), F32)

    for load in loads[:2]:
        load.wait()
    moduli[0, pl.ds(YL, ROWS), :] = lame_v[...].astype(F32) * time_step
    moduli[1, pl.ds(YL, ROWS), :] = shear_v[...].astype(F32) * time_step
    for load in loads[2:4]:
        load.wait()
    for side, rows in enumerate([end_rows, top_rows]):
        for n in range(3):
            y_send[side, n] = v_0[n, rows, :]
        y_send[side, 5] = moduli[1, rows, :]
    y_send[0, 3] = s_0[3, end_rows, :]
    y_send[0, 4] = s_0[5, end_rows, :]
    y_send[1, 3] = s_0[1, top_rows, :]
    y_send[1, 4] = moduli[0, top_rows, :]
    pl.semaphore_wait(barrier, 126 + 7 + 4)

    shears, both, only, one = pl.ds(3, 2), pl.ds(0, 2), pl.ds(0, 1), pl.ds(1, 1)
    copies = exchange(
        0,
        v_0,
        y_send,
        y_recv,
        [
            (s_0.at[shears, last], s_0.at[shears, below], (next_gx, gy)),
            (s_0.at[only, first], s_0.at[only, above], (prior_gx, gy)),
            (moduli.at[one, last], moduli.at[one, below], (next_gx, gy)),
            (moduli.at[both, first], moduli.at[both, above], (prior_gx, gy)),
        ],
    )
    stress_inside(v_0, s_0, s_1)
    arrive(0, copies, v_0, y_recv, 6)
    stress_rims(v_0, s_0, s_1, y_recv, 0)
    loads[4].wait()
    velocity_update(v_0, s_1, v_1)
    for side, rows in enumerate([end_rows, top_rows]):
        for n in range(3):
            y_send_2[side, n] = v_1[n, rows, :]
    copies = exchange(1, v_1, y_send_2, y_recv_2, [])
    stress_inside(v_1, s_1, s_1)
    arrive(1, copies, v_1, y_recv_2, 3)
    stress_rims(v_1, s_1, s_1, y_recv_2, 1)
    velocity_update(v_1, s_1, v_2)

    for load in loads[5:8]:
        load.wait()

    def narrow(n):
        return small_v[n, 0], small_v[n, 1]

    def wide(n):
        return large_v[n, 0], large_v[n, 1]

    turn_y = turns_v[0], turns_v[1]
    turn_x = turns_v[2], turns_v[3]
    mine = gy % 2 * 64 + gx

    def landed(ref, sem):
        pltpu.make_async_copy(ref, ref, sem).wait()

    def planes_of(value):
        return [lanes(rows_of(value, part), h) for part in range(2) for h in range(2)]

    for n, plane in enumerate(planes_of(z_forward(v_2[1, pl.ds(YL, ROWS), :], narrow(0)))):
        z_one[:, n, :] = plane

    def send_one(k, carry):
        other, device = in_plane(k, 1)
        send(z_one.at[other], x_recv.at[mine, 0], device, one_send.at[0], plane_recv.at[0])
        return carry

    lax.fori_loop(1, 64, send_one, 0)

    for slot, field in enumerate([0, 2]):
        value = z_forward(v_2[field, pl.ds(YL, ROWS), :], narrow(slot))
        for n, plane in enumerate(planes_of(value)):
            z_two[:, slot, n, :] = plane

    def send_two(k, carry):
        other, device = in_plane(k, 0)
        send(z_two.at[other], x_recv.at[mine], device, two_send.at[0], plane_recv.at[0])
        return carry

    lax.fori_loop(1, 64, send_two, 0)

    @pl.when(core == 0)
    def _():
        send_one(0, 0)
        x_recv[mine] = z_two[column]

    @pl.when(core == 1)
    def _():
        send_two(0, 0)
        x_recv[mine, 0] = z_one[column]

    @pl.when(core == 0)
    def _():
        landed(x_recv.at[pl.ds(0, 127)], plane_recv.at[0])

    @pl.when(core == 1)
    def _():
        landed(x_recv.at[pl.ds(0, 127), 0], plane_recv.at[0])

    fields = [
        [x_recv[pl.ds(64 * z, 64), slot, n, :] for n in range(4)]
        for z in range(2)
        for slot in range(2)
    ]
    pairs = x_forward(fields, narrow(4), [wide(2), wide(3)], *turn_x)
    alpha = waves[0]
    for z in range(2):
        for part in range(2):
            value = alpha * pairs[2 * z][part] + pairs[2 * z + 1][part]
            x_send[:, 2 * part + z] = value.reshape(8, 8, 256)

    def ring_exchange(sending, receiving, turn):
        def one(k, carry):
            other, device = in_ring(k)
            send(
                sending.at[other],
                receiving.at[place],
                device,
                ring_send.at[turn],
                ring_recv.at[turn],
            )
            return carry

        lax.fori_loop(1, 8, one, 0)
        receiving[place] = sending[place]
        landed(receiving.at[pl.ds(0, 7)], ring_recv.at[turn])

    ring_exchange(x_send, x_recv_2, 0)

    pairs = []
    for its_core in range(2):
        arrived = [
            x_recv_2[2 * x + its_core, 2 * part + z]
            for part in range(2)
            for x in range(4)
            for z in range(2)
        ]
        pairs.append(y_forward_left(jnp.concatenate(arrived, axis=0), narrow(2), *turn_y))
    joined, along_y = halves_product(pairs, wide(0))
    wave_y, inverse = waves[1], waves[2]
    phi = [(wave_y * along_y[part] + joined[part]) * inverse for part in range(2)]
    pairs = halves_product([phi, [wave_y * v for v in phi]], wide(1))
    for its_core in range(2):
        value = y_back_left(pairs[its_core], narrow(3), *turn_y)
        for part in range(2):
            for x in range(4):
                for z in range(2):
                    row = part * 64 + (2 * x + z) * 8
                    x_send_2[2 * x + its_core, 2 * part + z] = value[row : row + 8]
    ring_exchange(x_send_2, x_back, 1)

    pairs = []
    for z in range(2):
        pair = [x_back[:, 2 * part + z].reshape(64, 256) for part in range(2)]
        pairs += [[alpha * v for v in pair], pair]
    planes = x_backward(pairs, narrow(5), [wide(4), wide(5)], *turn_x)
    for z in range(2):
        for slot in range(2):
            for n in range(4):
                x_home[pl.ds(64 * z, 64), slot, n, :] = planes[2 * z + slot][n]

    @pl.when(core == 0)
    def _():
        def home(its_core):
            def one(k, carry):
                other, device = in_plane(k, its_core)
                source = x_home.at[other // 32 * 64 + device[0]]
                send(source, z_two_back.at[column], device, two_send.at[1], plane_recv.at[1])
                return carry

            return one

        lax.fori_loop(1, 64, home(0), 0)
        lax.fori_loop(0, 64, home(1), 0)
        z_two_back[column] = x_home[mine]

    @pl.when(core == 1)
    def _():
        def home(its_core):
            def one(k, carry):
                other, device = in_plane(k, its_core)
                source = x_home.at[other // 32 * 64 + device[0], 0]
                send(source, z_one_back.at[column], device, one_send.at[1], plane_recv.at[2])
                return carry

            return one

        lax.fori_loop(1, 64, home(1), 0)
        lax.fori_loop(0, 64, home(0), 0)
        z_one_back[column] = x_home[mine, 0]

    for load in loads[8:]:
        load.wait()

    @pl.when(core == 0)
    def _():
        landed(z_two_back.at[pl.ds(0, 63)], plane_recv.at[1])
        landed(z_one_back, plane_recv.at[2])

    @pl.when(core == 1)
    def _():
        landed(z_two_back, plane_recv.at[1])
        landed(z_one_back.at[pl.ds(0, 63)], plane_recv.at[2])

    def column_rows(planes):
        halves = [jnp.concatenate(planes[2 * p : 2 * p + 2], axis=1) for p in range(2)]
        return jnp.concatenate(halves, axis=0)

    gathered = [
        column_rows([z_two_back[:, 0, n, :] for n in range(4)]),
        column_rows([z_one_back[:, n, :] for n in range(4)]),
        column_rows([z_two_back[:, 1, n, :] for n in range(4)]),
    ]
    total_p = jnp.zeros((ROWS, NZ), F32)
    total_s = jnp.zeros((ROWS, NZ), F32)
    for field in range(3):
        p_field = z_back(gathered[field], narrow(7 if field == 2 else 6))
        s_field = v_2[field, pl.ds(YL, ROWS), :] - p_field
        total_p += source_p_v[field].astype(F32) * p_field
        total_s += source_s_v[field].astype(F32) * s_field
    image_p[...] = total_p
    image_s[...] = total_s

    for copy in sent:
        copy.wait_send()
    landed(x_send.at[pl.ds(0, 7)], ring_send.at[0])
    landed(x_send_2.at[pl.ds(0, 7)], ring_send.at[1])

    @pl.when(core == 0)
    def _():
        landed(z_two.at[pl.ds(0, 63)], two_send.at[0])
        landed(z_one, one_send.at[0])
        landed(x_home.at[pl.ds(0, 127)], two_send.at[1])

    @pl.when(core == 1)
    def _():
        landed(z_two, two_send.at[0])
        landed(z_one.at[pl.ds(0, 63)], one_send.at[0])
        landed(x_home.at[pl.ds(0, 127), 0], one_send.at[1])


def shards(small, large, turns, velocity, stress, lame, shear, buoy, source_p, source_s):
    in_place = pl.BlockSpec(memory_space=pltpu.HBM)
    padded = (XL + 2) * YL
    dma = pltpu.SemaphoreType.DMA
    scratch = [
        *[pltpu.VMEM((3, padded, NZ), F32)] * 3,
        *[pltpu.VMEM((6, padded, NZ), F32)] * 2,
        pltpu.VMEM((3, XL, NZ), F32),
        *[pltpu.VMEM((ROWS, NZ), BF16)] * 3,
        *[pltpu.VMEM((3, ROWS, NZ), BF16)] * 2,
        pltpu.VMEM(small.shape, BF16),
        pltpu.VMEM(large.shape, BF16),
        pltpu.VMEM(turns.shape, F32),
        pltpu.VMEM((2, padded, NZ), F32),
        *[pltpu.VMEM((2, 6, XL, NZ), F32)] * 2,
        *[pltpu.VMEM((2, 3, XL, NZ), F32)] * 2,
        pltpu.VMEM((2, 2, XL, NZ), F32),
        pltpu.VMEM((3, 64, 256), F32),
        pltpu.VMEM((64, 2, 4, 128), F32),
        pltpu.VMEM((64, 4, 128), F32),
        pltpu.VMEM((128, 2, 4, 128), F32),
        *[pltpu.VMEM((8, 4, 8, 256), F32)] * 3,
        pltpu.VMEM((64, 2, 4, 128), F32),
        pltpu.VMEM((64, 4, 128), F32),
        pltpu.VMEM((8, 4, 8, 256), F32),
        pltpu.VMEM((128, 2, 4, 128), F32),
        dma((10,)),
        dma((2, 10)),
        dma((2, 10)),
        dma((2,)),
        dma((2,)),
        dma((3,)),
        dma((2,)),
        dma((2,)),
    ]
    out = jax.ShapeDtypeStruct((ROWS, NZ), F32)
    outs = pl.pallas_call(
        kernel,
        out_shape=(out, out),
        in_specs=[in_place] * 10,
        out_specs=(pl.BlockSpec(memory_space=pltpu.VMEM),) * 2,
        scratch_shapes=scratch,
        compiler_params=pltpu.CompilerParams(
            collective_id=0, has_side_effects=True, vmem_limit_bytes=60 * 2**20
        ),
    )(
        velocity.reshape(3, ROWS, NZ),
        stress.reshape(6, ROWS, NZ),
        lame.reshape(ROWS, NZ),
        shear.reshape(ROWS, NZ),
        buoy.reshape(ROWS, NZ),
        source_p.reshape(3, ROWS, NZ),
        source_s.reshape(3, ROWS, NZ),
        small,
        large,
        turns,
    )
    return tuple(o.reshape(XL, YL, NZ) for o in outs)


def solution(mesh):
    small, large, turns = tables()

    def body(*blocks):
        return shards(jnp.asarray(small), jnp.asarray(large), jnp.asarray(turns), *blocks)

    in_specs = (
        P(None, "gx", "gy", None),
        P(None, "gx", "gy", None),
        P("gx", "gy", None),
        P("gx", "gy", None),
        P("gx", "gy", None),
        P(None, "gx", "gy", None),
        P(None, "gx", "gy", None),
    )
    out_specs = (P("gx", "gy", None), P("gx", "gy", None))
    return jax.shard_map(body, mesh=mesh, in_specs=in_specs, out_specs=out_specs, check_vma=False)
```

```python
import functools
import math

import jax
import jax.numpy as jnp
import numpy as np
from jax import lax
from jax.experimental import pallas as pl
from jax.experimental.pallas import tpu as pltpu
from jax.sharding import PartitionSpec as P

STEPS = 2
NX, NY, NZ = 512, 256, 128
GX, GY = 64, 8
XL, YL = NX // GX, NY // GY
ROWS = XL * YL
time_step = 0.2

MESH = pl.DeviceIdType.MESH
F32, BF16 = jnp.float32, jnp.bfloat16


def real_form(matrix):
    return np.block([[matrix.real, matrix.imag], [-matrix.imag, matrix.real]])


def left_form(matrix):
    return np.block([[matrix.real, -matrix.imag], [matrix.imag, matrix.real]])


def dft(length, sign):
    k = np.arange(length)
    return np.exp(sign * 2j * math.pi * (np.outer(k, k) % length) / length)


def tables():
    z = np.arange(NZ)
    forward_z = np.zeros((NZ, NZ))
    weighted_z = np.zeros((NZ, NZ))
    back_z = np.zeros((NZ, NZ))
    weighted_back = np.zeros((NZ, NZ))
    norm = 1.0 / (NX * NY * NZ)
    for column in range(NZ // 2):
        real_row, imag_row = column, NZ // 2 + column
        angle = 2 * math.pi * (column * z % NZ) / NZ
        cosine, sine = np.cos(angle), np.sin(angle)
        if column == 0:
            sign = 1.0 - 2.0 * (z % 2)
            forward_z[real_row], forward_z[imag_row] = 1.0, sign
            back_z[real_row], back_z[imag_row] = norm, norm * sign
        else:
            forward_z[real_row], forward_z[imag_row] = cosine, -sine
            back_z[real_row], back_z[imag_row] = 2 * norm * cosine, -2 * norm * sine
        weighted_z[real_row] = column * forward_z[real_row]
        weighted_z[imag_row] = column * forward_z[imag_row]
        weighted_back[real_row] = column * back_z[real_row]
        weighted_back[imag_row] = column * back_z[imag_row]

    per = NX // 64
    left_y = left_form(np.kron(dft(GY, -1), np.eye(per)))
    left_y_back = left_form(np.kron(dft(GY, 1), np.eye(per)))
    q1 = np.arange(64) // per
    yl = np.arange(ROWS) % YL
    turn_y = np.exp(-2j * math.pi * (np.outer(q1, yl) % NY) / NY)
    local_y = real_form(np.kron(np.eye(4), dft(YL, -1)))
    local_y_back = real_form(np.kron(np.eye(4), dft(YL, 1)))

    left_x = left_form(dft(GX, -1))
    left_x_back = left_form(dft(GX, 1))
    xl = np.arange(ROWS) // YL
    turn_x = np.exp(-2j * math.pi * (np.outer(np.arange(64), xl) % NX) / NX)
    local_x = []
    for a in range(2):
        small = np.diag(np.exp(-2j * math.pi * a * np.arange(4) / 8)) @ dft(4, -1)
        local_x.append(np.kron(small, np.eye(YL)))
    local_x_back = [real_form(m.conj().T) for m in local_x]
    local_x = [real_form(m) for m in local_x]

    def pair(stack):
        stack = np.stack(stack).astype(np.float32)
        high = stack.astype(BF16)
        low = (stack - high.astype(np.float32)).astype(BF16)
        return np.stack([high, low], axis=1)

    small = pair(
        [forward_z, weighted_z, left_y, left_y_back, left_x, left_x_back, back_z, weighted_back]
    )
    large = pair([local_y, local_y_back] + local_x + local_x_back)
    turns = np.stack([turn_y.real, turn_y.imag, turn_x.real, turn_x.imag]).astype(np.float32)
    return small, large, turns


def split(value):
    high = value.astype(BF16)
    return high, (value - high.astype(F32)).astype(BF16)


def product(left, right, dims):
    def one(a, b):
        return lax.dot_general(a, b, (dims, ((), ())), preferred_element_type=F32)

    return one(left[0], right[0]) + (one(left[0], right[1]) + one(left[1], right[0]))


NN = ((1,), (0,))
NT = ((1,), (1,))
TN = ((0,), (0,))


def matmul(left, right, dims=NN):
    left = left if isinstance(left, tuple) else split(left)
    right = right if isinstance(right, tuple) else split(right)
    return product(left, right, dims)


def turned(real, imag, cosine, sine, back):
    if back:
        return real * cosine + imag * sine, imag * cosine - real * sine
    return real * cosine - imag * sine, imag * cosine + real * sine


def lanes(value, half):
    return value[:, half * 128 : half * 128 + 128]


def z_forward(field, table):
    return matmul(table, field, NT)


def y_forward_left(arrived, left, cosine, sine):
    both = matmul(left, arrived)
    return turned(both[:64], both[64:], cosine, sine, False)


def halves_product(pairs, table):
    stacked = jnp.concatenate(
        [
            jnp.concatenate([lanes(re, h), lanes(im, h)], axis=1)
            for re, im in pairs
            for h in range(2)
        ],
        axis=0,
    )
    out = matmul(stacked, table)
    result = []
    for n in range(len(pairs)):
        rows = [out[(2 * n + h) * 64 : (2 * n + h) * 64 + 64] for h in range(2)]
        result.append(
            tuple(
                jnp.concatenate([r[:, part * 128 : part * 128 + 128] for r in rows], axis=1)
                for part in range(2)
            )
        )
    return result


def signed(positions, length):
    half = length // 2
    value = jnp.where(positions < half, positions, positions - length)
    return jnp.where(positions == half, 0, value).astype(F32)


def iota(axis):
    return lax.broadcasted_iota(jnp.int32, (64, 256), axis)


def wave_x_of(first, rows):
    lane = iota(1)
    return signed(first + rows + 64 * (lane // 128 + 2 * (lane % 128 // YL)), NX)


def waves_here(place, column):
    wave_x = wave_x_of(place * 8, iota(0) % 8)
    wave_y = signed(iota(0) // 8 + 8 * (iota(1) % YL), NY)
    wave_z = column.astype(F32)
    size = wave_x * wave_x + wave_y * wave_y + wave_z * wave_z
    return wave_y, 1.0 / jnp.maximum(size, 1.0)


def rows_of(value, n):
    return value[n * 64 : n * 64 + 64]


def x_forward(fields, left, local, cosine, sine):
    stacked = [
        jnp.concatenate([planes[h], planes[2 + h]], axis=0) for planes in fields for h in range(2)
    ]
    out = matmul(left, jnp.concatenate(stacked, axis=1))
    even, odd = [], []
    for n in range(len(fields)):
        block = out[:, n * 256 : n * 256 + 256]
        pair = turned(block[:64], block[64:], cosine, sine, False)
        even.append(jnp.concatenate([lanes(v, 0) + lanes(v, 1) for v in pair], axis=1))
        odd.append(jnp.concatenate([lanes(v, 0) - lanes(v, 1) for v in pair], axis=1))
    both = [matmul(jnp.concatenate(v, axis=0), t) for v, t in zip((even, odd), local)]
    return [
        [
            jnp.concatenate([lanes(rows_of(v, n), part) for v in both], axis=1)
            for part in range(2)
        ]
        for n in range(len(fields))
    ]


def x_backward(pairs, left, local, cosine, sine):
    zero, one = [
        matmul(
            jnp.concatenate(
                [jnp.concatenate([lanes(v, a) for v in pair], axis=1) for pair in pairs], axis=0
            ),
            local[a],
        )
        for a in range(2)
    ]
    stacked = []
    for n in range(len(pairs)):
        for h in range(2):
            even, odd = rows_of(zero, n), rows_of(one, n)
            both = even + odd if h == 0 else even - odd
            re, im = turned(
                lanes(both, 0), lanes(both, 1), lanes(cosine, h), lanes(sine, h), True
            )
            stacked.append(jnp.concatenate([re, im], axis=0))
    out = matmul(left, jnp.concatenate(stacked, axis=1))
    return [
        [lanes(rows_of(out, part), 2 * n + h) for part in range(2) for h in range(2)]
        for n in range(len(pairs))
    ]


def y_back_left(pair, left, cosine, sine):
    re, im = turned(pair[0], pair[1], cosine, sine, True)
    return matmul(left, jnp.concatenate([re, im], axis=0))


def z_back(arrived, table):
    return matmul(arrived, table, TN)


def kernel(
    velocity, stress, lame, shear, buoy, source_p, source_s, small, large, turns,
    image_p, image_s,
    v_0, v_1, v_2, s_0, s_1, rims, lame_v, shear_v, buoy_v, source_p_v, source_s_v,
    small_v, large_v, turns_v, moduli, y_send, y_recv, y_send_2, y_recv_2, corners,
    waves, z_two, z_one, x_recv, x_send, x_recv_2, x_send_2, z_two_back, z_one_back,
    x_back, x_home, load_sem, halo_send, halo_recv,
    two_send, one_send, plane_recv, ring_send, ring_recv,
):
    gx, gy = lax.axis_index("gx"), lax.axis_index("gy")

    barrier = pltpu.get_barrier_semaphore()

    def greet(device):
        pl.semaphore_signal(barrier, inc=1, device_id=device, device_id_type=MESH)

    core, place = gx % 2, gy // 2 * 2 + gx % 2
    column = gy % 2 * 32 + gx // 2

    def in_plane(k, its_core):
        other = (column + k) % 64
        return other, (other % 32 * 2 + its_core, gy // 2 * 2 + other // 32)

    def in_ring(k):
        other = (place + k) % 8
        return other, (gx // 2 * 2 + other % 2, other // 2 * 2 + gy % 2)

    def greet_plane(k, carry):
        greet(in_plane(k, 0)[1])
        greet(in_plane(k, 1)[1])
        return carry

    def greet_ring(k, carry):
        greet(in_ring(k)[1])
        return carry

    next_gx, prior_gx = lax.rem(gx + 1, GX), lax.rem(gx + GX - 1, GX)
    next_gy, prior_gy = lax.rem(gy + 1, GY), lax.rem(gy + GY - 1, GY)
    def interior(ref):
        return ref.at[:, pl.ds(YL, ROWS)]

    loads = [
        (lame, lame_v),
        (shear, shear_v),
        (velocity, interior(v_0)),
        (stress, interior(s_0)),
        (buoy, buoy_v),
        (small, small_v),
        (large, large_v),
        (turns, turns_v),
        (source_p, source_p_v),
        (source_s, source_s_v),
    ]
    loads = [pltpu.make_async_copy(a, b, load_sem.at[n]) for n, (a, b) in enumerate(loads)]
    for load in loads:
        load.start()
    lax.fori_loop(1, 64, greet_plane, 0)
    lax.fori_loop(1, 8, greet_ring, 0)
    greet((gx, next_gy))
    greet((gx, prior_gy))
    greet((next_gx, prior_gy))
    greet((prior_gx, next_gy))

    def send(source, target, device, send_sem, recv_sem):
        copy = pltpu.make_async_remote_copy(
            src_ref=source,
            dst_ref=target,
            send_sem=send_sem,
            recv_sem=recv_sem,
            device_id=device,
            device_id_type=MESH,
        )
        copy.start()
        return copy

    first, last = pl.ds(YL, YL), pl.ds(ROWS, YL)
    below, above = pl.ds(0, YL), pl.ds(ROWS + YL, YL)
    top_rows = pl.ds(YL, XL, stride=YL)
    end_rows = pl.ds(2 * YL - 1, XL, stride=YL)
    every = pl.ds(0, 3)
    sent = []

    def exchange(turn, v, sending, receiving, more):
        plan = [
            (sending.at[0], receiving.at[0], (gx, next_gy)),
            (sending.at[1], receiving.at[1], (gx, prior_gy)),
            (sending.at[0, 1], corners.at[turn, 0], (prior_gx, next_gy)),
            (sending.at[1, 0], corners.at[turn, 1], (next_gx, prior_gy)),
            (v.at[every, last], v.at[every, below], (next_gx, gy)),
            (v.at[every, first], v.at[every, above], (prior_gx, gy)),
        ] + more
        copies = [
            send(source, target, device, halo_send.at[turn, n], halo_recv.at[turn, n])
            for n, (source, target, device) in enumerate(plan)
        ]
        sent.extend(copies)
        return copies

    def arrive(turn, copies, v, receiving, fields):
        for copy in copies:
            copy.wait_recv()
        nothing = jnp.zeros((YL, NZ), F32)

        @pl.when(gx == 0)
        def _():
            for n in range(3):
                v[n, below, :] = nothing
            if turn == 0:
                s_0[3, below, :] = nothing
                s_0[4, below, :] = nothing
                moduli[1, below, :] = nothing
            corners[turn, 1] = nothing[:XL]

        @pl.when(gx == GX - 1)
        def _():
            for n in range(3):
                v[n, above, :] = nothing
            if turn == 0:
                s_0[0, above, :] = nothing
                moduli[0, above, :] = nothing
                moduli[1, above, :] = nothing
            corners[turn, 0] = nothing[:XL]

        @pl.when(gy == 0)
        def _():
            for n in range(fields):
                receiving[0, n] = nothing[:XL]
            corners[turn, 0] = nothing[:XL]

        @pl.when(gy == GY - 1)
        def _():
            for n in range(fields):
                receiving[1, n] = nothing[:XL]
            corners[turn, 1] = nothing[:XL]

    def at_row(f, row):
        return lax.broadcasted_iota(jnp.int32, f.shape, 0) == row

    def at_lane(f, lane):
        return lax.broadcasted_iota(jnp.int32, f.shape, 1) == lane

    def next_z(f):
        return jnp.where(at_lane(f, NZ - 1), 0.0, pltpu.roll(f, NZ - 1, 1))

    def prior_z(f):
        return jnp.where(at_lane(f, 0), 0.0, pltpu.roll(f, 1, 1))

    def next_row(f, rim):
        return jnp.where(at_row(f, f.shape[0] - 1), rim, pltpu.roll(f, f.shape[0] - 1, 0))

    def prior_row(f, rim):
        return jnp.where(at_row(f, 0), rim, pltpu.roll(f, 1, 0))

    def plane_at(i):
        return i if isinstance(i, int) else pl.multiple_of(i, YL)

    def over_planes(plane):
        plane(0, False, True)

        def middle(i, carry):
            plane(i, True, True)
            return carry

        lax.fori_loop(1, XL - 1, middle, 0)
        plane(XL - 1, True, False)

    def stress_inside(v, s_in, s_out):
        def plane(i, has_before, has_after):
            here = pl.ds(plane_at((i + 1) * YL), YL)
            before = pl.ds(plane_at(i * YL), YL)
            after = pl.ds(plane_at((i + 2) * YL), YL)
            v_x, v_y, v_z = v[0, here, :], v[1, here, :], v[2, here, :]
            lam, mu = moduli[0, here, :], moduli[1, here, :]
            e_x = v_x - v[0, before, :] if has_before else v_x
            e_y = v_y - prior_row(v_y, 0.0)
            e_z = v_z - prior_z(v_z)
            x_y = v[1, after, :] - v_y if has_after else -v_y
            x_z = v[2, after, :] - v_z if has_after else -v_z
            volume = lam * (e_x + e_y + e_z)
            twice = 2.0 * mu
            s_out[0, here, :] = s_in[0, here, :] + (volume + twice * e_x)
            s_out[1, here, :] = s_in[1, here, :] + (volume + twice * e_y)
            s_out[2, here, :] = s_in[2, here, :] + (volume + twice * e_z)
            s_out[3, here, :] = s_in[3, here, :] + mu * ((next_row(v_x, 0.0) - v_x) + x_y)
            s_out[4, here, :] = s_in[4, here, :] + mu * ((next_z(v_x) - v_x) + x_z)
            s_out[5, here, :] = s_in[5, here, :] + mu * (
                (next_z(v_y) - v_y) + (next_row(v_z, 0.0) - v_z)
            )

        over_planes(plane)

    def stress_rims(v, s_in, s_out, received, turn):
        prior_side = [received[0, n] for n in range(3)]
        next_side = [received[1, n] for n in range(3)]
        corner_y = corners[turn, 0, pl.ds(0, 1), :]
        corner_x = corners[turn, 1, pl.ds(XL - 1, 1), :]

        gone = v[0, below, :]
        lam, mu = moduli[0, first, :], moduli[1, first, :]
        s_out[0, first, :] -= (lam + 2.0 * mu) * gone
        s_out[1, first, :] -= lam * gone
        s_out[2, first, :] -= lam * gone
        mu = moduli[1, last, :]
        s_out[3, last, :] += mu * v[1, above, :]
        s_out[4, last, :] += mu * v[2, above, :]

        gone = prior_side[1]
        lam, mu = moduli[0, top_rows, :], moduli[1, top_rows, :]
        s_out[0, top_rows, :] -= lam * gone
        s_out[1, top_rows, :] -= (lam + 2.0 * mu) * gone
        s_out[2, top_rows, :] -= lam * gone
        mu = moduli[1, end_rows, :]
        s_out[3, end_rows, :] += mu * next_side[0]
        s_out[5, end_rows, :] += mu * next_side[2]

        v_x, v_y, v_z = v[0, above, :], v[1, above, :], v[2, above, :]
        lam, mu = moduli[0, above, :], moduli[1, above, :]
        e_x = v_x - v[0, last, :]
        e_y = v_y - prior_row(v_y, corner_y)
        e_z = v_z - prior_z(v_z)
        s_out[0, above, :] = s_in[0, above, :] + (lam * (e_x + e_y + e_z) + 2.0 * mu * e_x)

        v_x, v_y, v_z = v[0, below, :], v[1, below, :], v[2, below, :]
        mu = moduli[1, below, :]
        s_out[3, below, :] = s_in[3, below, :] + mu * (
            (next_row(v_x, corner_x) - v_x) + (v[1, first, :] - v_y)
        )
        s_out[4, below, :] = s_in[4, below, :] + mu * (
            (next_z(v_x) - v_x) + (v[2, first, :] - v_z)
        )

        v_x, v_y, v_z = next_side
        lam, mu = y_recv[1, 4], y_recv[1, 5]
        e_x = v_x - prior_row(v_x, corner_x)
        e_y = v_y - v[1, end_rows, :]
        e_z = v_z - prior_z(v_z)
        old = y_recv[1, 3] if turn == 0 else rims[0]
        rims[0] = old + (lam * (e_x + e_y + e_z) + 2.0 * mu * e_y)

        v_x, v_y, v_z = prior_side
        mu = y_recv[0, 5]
        old = y_recv[0, 3] if turn == 0 else rims[1]
        rims[1] = old + mu * ((v[0, top_rows, :] - v_x) + (next_row(v_y, corner_y) - v_y))
        old = y_recv[0, 4] if turn == 0 else rims[2]
        rims[2] = old + mu * ((next_z(v_y) - v_y) + (v[2, top_rows, :] - v_z))

    def velocity_plane(v_in, s, v_out, i):
        here = pl.ds(plane_at((i + 1) * YL), YL)
        before = pl.ds(plane_at(i * YL), YL)
        after = pl.ds(plane_at((i + 2) * YL), YL)
        rim_yy, rim_xy, rim_yz = 0.0, 0.0, 0.0
        if isinstance(i, int):
            rim_yy, rim_xy, rim_yz = [rims[n, pl.ds(i, 1), :] for n in range(3)]
        b = moduli[2, here, :]
        xx, yy, zz = s[0, here, :], s[1, here, :], s[2, here, :]
        xy, xz, yz = s[3, here, :], s[4, here, :], s[5, here, :]
        v_out[0, here, :] = v_in[0, here, :] + b * (
            (s[0, after, :] - xx) + (xy - prior_row(xy, rim_xy)) + (xz - prior_z(xz))
        )
        v_out[1, here, :] = v_in[1, here, :] + b * (
            (xy - s[3, before, :]) + (next_row(yy, rim_yy) - yy) + (yz - prior_z(yz))
        )
        v_out[2, here, :] = v_in[2, here, :] + b * (
            (xz - s[4, before, :]) + (yz - prior_row(yz, rim_yz)) + (next_z(zz) - zz)
        )

    def velocity_inside(v_in, s, v_out):
        def middle(i, carry):
            velocity_plane(v_in, s, v_out, i)
            return carry

        lax.fori_loop(1, XL - 1, middle, 0)

    def velocity_rims(v_in, s, v_out):
        velocity_plane(v_in, s, v_out, 0)
        velocity_plane(v_in, s, v_out, XL - 1)
        for row in (0, YL - 1):
            rows = pl.ds(YL + row, XL, stride=YL)
            beside = pl.ds(YL + row + (1 if row == 0 else -1), XL, stride=YL)
            over, under = pl.ds(ROWS + YL + row, 1), pl.ds(row, 1)
            b = moduli[2, rows, :]
            xx, yy, zz = s[0, rows, :], s[1, rows, :], s[2, rows, :]
            xy, xz, yz = s[3, rows, :], s[4, rows, :], s[5, rows, :]
            if row == 0:
                xy_prior, yz_prior, yy_next = rims[1], rims[2], s[1, beside, :]
            else:
                xy_prior, yz_prior, yy_next = s[3, beside, :], s[5, beside, :], rims[0]
            v_out[0, rows, :] = v_in[0, rows, :] + b * (
                (next_row(xx, s[0, over, :]) - xx) + (xy - xy_prior) + (xz - prior_z(xz))
            )
            v_out[1, rows, :] = v_in[1, rows, :] + b * (
                (xy - prior_row(xy, s[3, under, :])) + (yy_next - yy) + (yz - prior_z(yz))
            )
            v_out[2, rows, :] = v_in[2, rows, :] + b * (
                (xz - prior_row(xz, s[4, under, :])) + (yz - yz_prior) + (next_z(zz) - zz)
            )

    wave_x = wave_x_of(0, iota(0))
    waves[0] = jnp.where(core == 0, wave_x, 1.0)
    waves[1], waves[2] = waves_here(place, column)

    @pl.when(core == 1)
    def _():
        x_recv[:, 1] = jnp.zeros((128, 4, 128), F32)

    for load in loads[:2]:
        load.wait()
    moduli[0, pl.ds(YL, ROWS), :] = lame_v[...].astype(F32) * time_step
    moduli[1, pl.ds(YL, ROWS), :] = shear_v[...].astype(F32) * time_step
    for load in loads[2:4]:
        load.wait()
    for side, rows in enumerate([end_rows, top_rows]):
        for n in range(3):
            y_send[side, n] = v_0[n, rows, :]
        y_send[side, 5] = moduli[1, rows, :]
    y_send[0, 3] = s_0[3, end_rows, :]
    y_send[0, 4] = s_0[5, end_rows, :]
    y_send[1, 3] = s_0[1, top_rows, :]
    y_send[1, 4] = moduli[0, top_rows, :]
    pl.semaphore_wait(barrier, 126 + 7 + 4)

    shears, both, only, one = pl.ds(3, 2), pl.ds(0, 2), pl.ds(0, 1), pl.ds(1, 1)
    copies = exchange(
        0,
        v_0,
        y_send,
        y_recv,
        [
            (s_0.at[shears, last], s_0.at[shears, below], (next_gx, gy)),
            (s_0.at[only, first], s_0.at[only, above], (prior_gx, gy)),
            (moduli.at[one, last], moduli.at[one, below], (next_gx, gy)),
            (moduli.at[both, first], moduli.at[both, above], (prior_gx, gy)),
        ],
    )
    stress_inside(v_0, s_0, s_1)
    loads[4].wait()
    moduli[2, pl.ds(YL, ROWS), :] = buoy_v[...].astype(F32) * time_step
    velocity_inside(v_0, s_1, v_1)
    arrive(0, copies, v_0, y_recv, 6)
    stress_rims(v_0, s_0, s_1, y_recv, 0)
    velocity_rims(v_0, s_1, v_1)
    for side, rows in enumerate([end_rows, top_rows]):
        for n in range(3):
            y_send_2[side, n] = v_1[n, rows, :]
    copies = exchange(1, v_1, y_send_2, y_recv_2, [])
    stress_inside(v_1, s_1, s_1)
    velocity_inside(v_1, s_1, v_2)
    arrive(1, copies, v_1, y_recv_2, 3)
    stress_rims(v_1, s_1, s_1, y_recv_2, 1)
    velocity_rims(v_1, s_1, v_2)

    for load in loads[5:8]:
        load.wait()

    def narrow(n):
        return small_v[n, 0], small_v[n, 1]

    def wide(n):
        return large_v[n, 0], large_v[n, 1]

    turn_y = turns_v[0], turns_v[1]
    turn_x = turns_v[2], turns_v[3]
    mine = gy % 2 * 64 + gx

    def landed(ref, sem):
        pltpu.make_async_copy(ref, ref, sem).wait()

    def planes_of(value):
        return [lanes(rows_of(value, part), h) for part in range(2) for h in range(2)]

    for n, plane in enumerate(planes_of(z_forward(v_2[1, pl.ds(YL, ROWS), :], narrow(0)))):
        z_one[:, n, :] = plane

    def send_one(k, carry):
        other, device = in_plane(k, 1)
        send(z_one.at[other], x_recv.at[mine, 0], device, one_send.at[0], plane_recv.at[0])
        return carry

    lax.fori_loop(1, 64, send_one, 0)

    for slot, field in enumerate([0, 2]):
        value = z_forward(v_2[field, pl.ds(YL, ROWS), :], narrow(slot))
        for n, plane in enumerate(planes_of(value)):
            z_two[:, slot, n, :] = plane

    def send_two(k, carry):
        other, device = in_plane(k, 0)
        send(z_two.at[other], x_recv.at[mine], device, two_send.at[0], plane_recv.at[0])
        return carry

    lax.fori_loop(1, 64, send_two, 0)

    @pl.when(core == 0)
    def _():
        send_one(0, 0)
        x_recv[mine] = z_two[column]

    @pl.when(core == 1)
    def _():
        send_two(0, 0)
        x_recv[mine, 0] = z_one[column]

    @pl.when(core == 0)
    def _():
        landed(x_recv.at[pl.ds(0, 127)], plane_recv.at[0])

    @pl.when(core == 1)
    def _():
        landed(x_recv.at[pl.ds(0, 127), 0], plane_recv.at[0])

    fields = [
        [x_recv[pl.ds(64 * z, 64), slot, n, :] for n in range(4)]
        for z in range(2)
        for slot in range(2)
    ]
    pairs = x_forward(fields, narrow(4), [wide(2), wide(3)], *turn_x)
    alpha = waves[0]
    for z in range(2):
        for part in range(2):
            value = alpha * pairs[2 * z][part] + pairs[2 * z + 1][part]
            x_send[:, 2 * part + z] = value.reshape(8, 8, 256)

    def ring_exchange(sending, receiving, turn):
        def one(k, carry):
            other, device = in_ring(k)
            send(
                sending.at[other],
                receiving.at[place],
                device,
                ring_send.at[turn],
                ring_recv.at[turn],
            )
            return carry

        lax.fori_loop(1, 8, one, 0)
        receiving[place] = sending[place]
        landed(receiving.at[pl.ds(0, 7)], ring_recv.at[turn])

    ring_exchange(x_send, x_recv_2, 0)

    pairs = []
    for its_core in range(2):
        arrived = [
            x_recv_2[2 * x + its_core, 2 * part + z]
            for part in range(2)
            for x in range(4)
            for z in range(2)
        ]
        pairs.append(y_forward_left(jnp.concatenate(arrived, axis=0), narrow(2), *turn_y))
    joined, along_y = halves_product(pairs, wide(0))
    wave_y, inverse = waves[1], waves[2]
    phi = [(wave_y * along_y[part] + joined[part]) * inverse for part in range(2)]
    pairs = halves_product([phi, [wave_y * v for v in phi]], wide(1))
    for its_core in range(2):
        value = y_back_left(pairs[its_core], narrow(3), *turn_y)
        for part in range(2):
            for x in range(4):
                for z in range(2):
                    row = part * 64 + (2 * x + z) * 8
                    x_send_2[2 * x + its_core, 2 * part + z] = value[row : row + 8]
    ring_exchange(x_send_2, x_back, 1)

    def home(z, its_core, wide_one):
        def one(k, carry):
            chip = (gx // 2 + k) % 32
            device = (chip * 2 + its_core, gy // 2 * 2 + z)
            if wide_one:
                source = x_home.at[z * 64 + device[0]]
                send(source, z_two_back.at[column], device, two_send.at[1], plane_recv.at[1])
            else:
                source = x_home.at[z * 64 + device[0], 0]
                send(source, z_one_back.at[column], device, one_send.at[1], plane_recv.at[2])
            return carry

        return one

    for z in range(2):
        pair = [x_back[:, 2 * part + z].reshape(64, 256) for part in range(2)]
        pairs = [[alpha * v for v in pair], pair]
        planes = x_backward(pairs, narrow(5), [wide(4), wide(5)], *turn_x)
        for slot in range(2):
            for n in range(4):
                x_home[pl.ds(64 * z, 64), slot, n, :] = planes[slot][n]
        for its_core in range(2):

            @pl.when(core == its_core)
            def _():
                same, other = home(z, its_core, its_core == 0), home(z, 1 - its_core, its_core == 0)
                lax.fori_loop(1, 32, same, 0)
                lax.fori_loop(1, 32, other, 0)
                other(0, 0)

                @pl.when(gy % 2 != z)
                def _():
                    same(0, 0)

    @pl.when(core == 0)
    def _():
        z_two_back[column] = x_home[mine]

    @pl.when(core == 1)
    def _():
        z_one_back[column] = x_home[mine, 0]

    for load in loads[8:]:
        load.wait()

    def column_rows(planes):
        halves = [jnp.concatenate(planes[2 * p : 2 * p + 2], axis=1) for p in range(2)]
        return jnp.concatenate(halves, axis=0)

    total_p = jnp.zeros((ROWS, NZ), F32)
    total_s = jnp.zeros((ROWS, NZ), F32)
    for field in (1, 0, 2):
        if field == 1:

            @pl.when(core == 0)
            def _():
                landed(z_one_back, plane_recv.at[2])

            @pl.when(core == 1)
            def _():
                landed(z_one_back.at[pl.ds(0, 63)], plane_recv.at[2])

            planes = [z_one_back[:, n, :] for n in range(4)]
        else:
            if field == 0:

                @pl.when(core == 0)
                def _():
                    landed(z_two_back.at[pl.ds(0, 63)], plane_recv.at[1])

                @pl.when(core == 1)
                def _():
                    landed(z_two_back, plane_recv.at[1])

            planes = [z_two_back[:, field // 2, n, :] for n in range(4)]
        p_field = z_back(column_rows(planes), narrow(7 if field == 2 else 6))
        s_field = v_2[field, pl.ds(YL, ROWS), :] - p_field
        total_p += source_p_v[field].astype(F32) * p_field
        total_s += source_s_v[field].astype(F32) * s_field
    image_p[...] = total_p
    image_s[...] = total_s

    for copy in sent:
        copy.wait_send()
    landed(x_send.at[pl.ds(0, 7)], ring_send.at[0])
    landed(x_send_2.at[pl.ds(0, 7)], ring_send.at[1])

    @pl.when(core == 0)
    def _():
        landed(z_two.at[pl.ds(0, 63)], two_send.at[0])
        landed(z_one, one_send.at[0])
        landed(x_home.at[pl.ds(0, 127)], two_send.at[1])

    @pl.when(core == 1)
    def _():
        landed(z_two, two_send.at[0])
        landed(z_one.at[pl.ds(0, 63)], one_send.at[0])
        landed(x_home.at[pl.ds(0, 127), 0], one_send.at[1])


def shards(small, large, turns, velocity, stress, lame, shear, buoy, source_p, source_s):
    in_place = pl.BlockSpec(memory_space=pltpu.HBM)
    padded = (XL + 2) * YL
    dma = pltpu.SemaphoreType.DMA
    scratch = [
        *[pltpu.VMEM((3, padded, NZ), F32)] * 3,
        *[pltpu.VMEM((6, padded, NZ), F32)] * 2,
        pltpu.VMEM((3, XL, NZ), F32),
        *[pltpu.VMEM((ROWS, NZ), BF16)] * 3,
        *[pltpu.VMEM((3, ROWS, NZ), BF16)] * 2,
        pltpu.VMEM(small.shape, BF16),
        pltpu.VMEM(large.shape, BF16),
        pltpu.VMEM(turns.shape, F32),
        pltpu.VMEM((3, padded, NZ), F32),
        *[pltpu.VMEM((2, 6, XL, NZ), F32)] * 2,
        *[pltpu.VMEM((2, 3, XL, NZ), F32)] * 2,
        pltpu.VMEM((2, 2, XL, NZ), F32),
        pltpu.VMEM((3, 64, 256), F32),
        pltpu.VMEM((64, 2, 4, 128), F32),
        pltpu.VMEM((64, 4, 128), F32),
        pltpu.VMEM((128, 2, 4, 128), F32),
        *[pltpu.VMEM((8, 4, 8, 256), F32)] * 3,
        pltpu.VMEM((64, 2, 4, 128), F32),
        pltpu.VMEM((64, 4, 128), F32),
        pltpu.VMEM((8, 4, 8, 256), F32),
        pltpu.VMEM((128, 2, 4, 128), F32),
        dma((10,)),
        dma((2, 10)),
        dma((2, 10)),
        dma((2,)),
        dma((2,)),
        dma((3,)),
        dma((2,)),
        dma((2,)),
    ]
    out = jax.ShapeDtypeStruct((ROWS, NZ), F32)
    outs = pl.pallas_call(
        kernel,
        out_shape=(out, out),
        in_specs=[in_place] * 10,
        out_specs=(pl.BlockSpec(memory_space=pltpu.VMEM),) * 2,
        scratch_shapes=scratch,
        compiler_params=pltpu.CompilerParams(
            collective_id=0, has_side_effects=True, vmem_limit_bytes=60 * 2**20
        ),
    )(
        velocity.reshape(3, ROWS, NZ),
        stress.reshape(6, ROWS, NZ),
        lame.reshape(ROWS, NZ),
        shear.reshape(ROWS, NZ),
        buoy.reshape(ROWS, NZ),
        source_p.reshape(3, ROWS, NZ),
        source_s.reshape(3, ROWS, NZ),
        small,
        large,
        turns,
    )
    return tuple(o.reshape(XL, YL, NZ) for o in outs)


def solution(mesh):
    small, large, turns = tables()

    def body(*blocks):
        return shards(jnp.asarray(small), jnp.asarray(large), jnp.asarray(turns), *blocks)

    in_specs = (
        P(None, "gx", "gy", None),
        P(None, "gx", "gy", None),
        P("gx", "gy", None),
        P("gx", "gy", None),
        P("gx", "gy", None),
        P(None, "gx", "gy", None),
        P(None, "gx", "gy", None),
    )
    out_specs = (P("gx", "gy", None), P("gx", "gy", None))
    return jax.shard_map(body, mesh=mesh, in_specs=in_specs, out_specs=out_specs, check_vma=False)
```

```python
import functools
import math

import jax
import jax.numpy as jnp
import numpy as np
from jax import lax
from jax.experimental import pallas as pl
from jax.experimental.pallas import tpu as pltpu
from jax.sharding import PartitionSpec as P

STEPS = 2
NX, NY, NZ = 512, 256, 128
GX, GY = 64, 8
XL, YL = NX // GX, NY // GY
ROWS = XL * YL
time_step = 0.2

MESH = pl.DeviceIdType.MESH
F32, BF16 = jnp.float32, jnp.bfloat16


def real_form(matrix):
    return np.block([[matrix.real, matrix.imag], [-matrix.imag, matrix.real]])


def left_form(matrix):
    return np.block([[matrix.real, -matrix.imag], [matrix.imag, matrix.real]])


def dft(length, sign):
    k = np.arange(length)
    return np.exp(sign * 2j * math.pi * (np.outer(k, k) % length) / length)


def tables():
    z = np.arange(NZ)
    forward_z = np.zeros((NZ, NZ))
    weighted_z = np.zeros((NZ, NZ))
    back_z = np.zeros((NZ, NZ))
    weighted_back = np.zeros((NZ, NZ))
    norm = 1.0 / (NX * NY * NZ)
    for column in range(NZ // 2):
        real_row, imag_row = column, NZ // 2 + column
        angle = 2 * math.pi * (column * z % NZ) / NZ
        cosine, sine = np.cos(angle), np.sin(angle)
        if column == 0:
            sign = 1.0 - 2.0 * (z % 2)
            forward_z[real_row], forward_z[imag_row] = 1.0, sign
            back_z[real_row], back_z[imag_row] = norm, norm * sign
        else:
            forward_z[real_row], forward_z[imag_row] = cosine, -sine
            back_z[real_row], back_z[imag_row] = 2 * norm * cosine, -2 * norm * sine
        weighted_z[real_row] = column * forward_z[real_row]
        weighted_z[imag_row] = column * forward_z[imag_row]
        weighted_back[real_row] = column * back_z[real_row]
        weighted_back[imag_row] = column * back_z[imag_row]

    per = NX // 64
    left_y = left_form(np.kron(dft(GY, -1), np.eye(per)))
    left_y_back = left_form(np.kron(dft(GY, 1), np.eye(per)))
    q1 = np.arange(64) // per
    yl = np.arange(ROWS) % YL
    turn_y = np.exp(-2j * math.pi * (np.outer(q1, yl) % NY) / NY)
    local_y = real_form(np.kron(np.eye(4), dft(YL, -1)))
    local_y_back = real_form(np.kron(np.eye(4), dft(YL, 1)))

    left_x = left_form(dft(GX, -1))
    left_x_back = left_form(dft(GX, 1))
    xl = np.arange(ROWS) // YL
    turn_x = np.exp(-2j * math.pi * (np.outer(np.arange(64), xl) % NX) / NX)
    local_x = []
    for a in range(2):
        small = np.diag(np.exp(-2j * math.pi * a * np.arange(4) / 8)) @ dft(4, -1)
        local_x.append(np.kron(small, np.eye(YL)))
    local_x_back = [real_form(m.conj().T) for m in local_x]
    local_x = [real_form(m) for m in local_x]

    def pair(stack):
        stack = np.stack(stack).astype(np.float32)
        high = stack.astype(BF16)
        low = (stack - high.astype(np.float32)).astype(BF16)
        return np.stack([high, low], axis=1)

    small = pair(
        [forward_z, weighted_z, left_y, left_y_back, left_x, left_x_back, back_z, weighted_back]
    )
    large = pair([local_y, local_y_back] + local_x + local_x_back)
    turns = np.stack([turn_y.real, turn_y.imag, turn_x.real, turn_x.imag]).astype(np.float32)
    return small, large, turns


def split(value):
    high = value.astype(BF16)
    return high, (value - high.astype(F32)).astype(BF16)


def product(left, right, dims):
    def one(a, b):
        return lax.dot_general(a, b, (dims, ((), ())), preferred_element_type=F32)

    return one(left[0], right[0]) + (one(left[0], right[1]) + one(left[1], right[0]))


NN = ((1,), (0,))
NT = ((1,), (1,))
TN = ((0,), (0,))


def matmul(left, right, dims=NN):
    left = left if isinstance(left, tuple) else split(left)
    right = right if isinstance(right, tuple) else split(right)
    return product(left, right, dims)


def turned(real, imag, cosine, sine, back):
    if back:
        return real * cosine + imag * sine, imag * cosine - real * sine
    return real * cosine - imag * sine, imag * cosine + real * sine


def lanes(value, half):
    return value[:, half * 128 : half * 128 + 128]


def z_forward(field, table):
    return matmul(table, field, NT)


def signed(positions, length):
    half = length // 2
    value = jnp.where(positions < half, positions, positions - length)
    return jnp.where(positions == half, 0, value).astype(F32)


def iota(axis):
    return lax.broadcasted_iota(jnp.int32, (64, 256), axis)


def wave_x_of(first, rows):
    lane = iota(1)
    return signed(first + rows + 64 * (lane // 128 + 2 * (lane % 128 // YL)), NX)


def waves_here(place, column):
    wave_x = wave_x_of(place * 8, iota(0) % 8)
    wave_y = signed(iota(0) // 8 + 8 * (iota(1) % YL), NY)
    wave_z = column.astype(F32)
    size = wave_x * wave_x + wave_y * wave_y + wave_z * wave_z
    return wave_y, 1.0 / jnp.maximum(size, 1.0)


def rows_of(value, n):
    return value[n * 64 : n * 64 + 64]


def x_forward(fields, left, cosine, sine):
    stacked = [
        jnp.concatenate([planes[h], planes[2 + h]], axis=0) for planes in fields for h in range(2)
    ]
    out = matmul(left, jnp.concatenate(stacked, axis=1))
    even, odd = [], []
    for n in range(len(fields)):
        block = out[:, n * 256 : n * 256 + 256]
        pair = turned(block[:64], block[64:], cosine, sine, False)
        even.append(jnp.concatenate([lanes(v, 0) + lanes(v, 1) for v in pair], axis=1))
        odd.append(jnp.concatenate([lanes(v, 0) - lanes(v, 1) for v in pair], axis=1))
    return [jnp.concatenate(v, axis=0) for v in (even, odd)]


def x_backward(zero, one, left, cosine, sine):
    count = zero.shape[0] // 64
    stacked = []
    for n in range(count):
        for h in range(2):
            even, odd = rows_of(zero, n), rows_of(one, n)
            both = even + odd if h == 0 else even - odd
            re, im = turned(
                lanes(both, 0), lanes(both, 1), lanes(cosine, h), lanes(sine, h), True
            )
            stacked.append(jnp.concatenate([re, im], axis=0))
    out = matmul(left, jnp.concatenate(stacked, axis=1))
    return [
        [lanes(rows_of(out, part), 2 * n + h) for part in range(2) for h in range(2)]
        for n in range(count)
    ]


def z_back(arrived, table):
    return matmul(arrived, table, TN)


def kernel(
    velocity, stress, lame, shear, buoy, source_p, source_s, small, large, turns,
    image_p, image_s,
    v_0, v_1, v_2, s_0, s_1, rims, lame_v, shear_v, buoy_v, source_p_v, source_s_v,
    small_v, large_v, turns_v, moduli, y_send, y_recv, y_send_2, y_recv_2, corners,
    waves, z_two, z_one, x_recv, x_send, x_recv_2, x_send_2, z_two_back, z_one_back,
    x_back, x_home, load_sem, halo_send, halo_recv,
    two_send, one_send, plane_recv, ring_send, ring_recv,
):
    gx, gy = lax.axis_index("gx"), lax.axis_index("gy")

    barrier = pltpu.get_barrier_semaphore()

    def greet(device):
        pl.semaphore_signal(barrier, inc=1, device_id=device, device_id_type=MESH)

    core, place = gx % 2, gy // 2 * 2 + gx % 2
    column = gy % 2 * 32 + gx // 2

    def in_plane(k, its_core):
        other = (column + k) % 64
        return other, (other % 32 * 2 + its_core, gy // 2 * 2 + other // 32)

    def in_ring(k):
        other = (place + k) % 8
        return other, (gx // 2 * 2 + other % 2, other // 2 * 2 + gy % 2)

    def greet_plane(k, carry):
        greet(in_plane(k, 0)[1])
        greet(in_plane(k, 1)[1])
        return carry

    def greet_ring(k, carry):
        greet(in_ring(k)[1])
        return carry

    next_gx, prior_gx = lax.rem(gx + 1, GX), lax.rem(gx + GX - 1, GX)
    next_gy, prior_gy = lax.rem(gy + 1, GY), lax.rem(gy + GY - 1, GY)
    def interior(ref):
        return ref.at[:, pl.ds(YL, ROWS)]

    loads = [
        (lame, lame_v),
        (shear, shear_v),
        (velocity, interior(v_0)),
        (stress, interior(s_0)),
        (buoy, buoy_v),
        (small, small_v),
        (large, large_v),
        (turns, turns_v),
        (source_p, source_p_v),
        (source_s, source_s_v),
    ]
    loads = [pltpu.make_async_copy(a, b, load_sem.at[n]) for n, (a, b) in enumerate(loads)]
    for load in loads:
        load.start()
    lax.fori_loop(1, 64, greet_plane, 0)
    lax.fori_loop(1, 8, greet_ring, 0)
    greet((gx, next_gy))
    greet((gx, prior_gy))
    greet((next_gx, prior_gy))
    greet((prior_gx, next_gy))

    def send(source, target, device, send_sem, recv_sem):
        copy = pltpu.make_async_remote_copy(
            src_ref=source,
            dst_ref=target,
            send_sem=send_sem,
            recv_sem=recv_sem,
            device_id=device,
            device_id_type=MESH,
        )
        copy.start()
        return copy

    first, last = pl.ds(YL, YL), pl.ds(ROWS, YL)
    below, above = pl.ds(0, YL), pl.ds(ROWS + YL, YL)
    top_rows = pl.ds(YL, XL, stride=YL)
    end_rows = pl.ds(2 * YL - 1, XL, stride=YL)
    every = pl.ds(0, 3)
    sent = []

    def exchange(turn, v, sending, receiving, more):
        plan = [
            (sending.at[0], receiving.at[0], (gx, next_gy)),
            (sending.at[1], receiving.at[1], (gx, prior_gy)),
            (sending.at[0, 1], corners.at[turn, 0], (prior_gx, next_gy)),
            (sending.at[1, 0], corners.at[turn, 1], (next_gx, prior_gy)),
            (v.at[every, last], v.at[every, below], (next_gx, gy)),
            (v.at[every, first], v.at[every, above], (prior_gx, gy)),
        ] + more
        copies = [
            send(source, target, device, halo_send.at[turn, n], halo_recv.at[turn, n])
            for n, (source, target, device) in enumerate(plan)
        ]
        sent.extend(copies)
        return copies

    def arrive(turn, copies, v, receiving, fields):
        for copy in copies:
            copy.wait_recv()
        nothing = jnp.zeros((YL, NZ), F32)

        @pl.when(gx == 0)
        def _():
            for n in range(3):
                v[n, below, :] = nothing
            if turn == 0:
                s_0[3, below, :] = nothing
                s_0[4, below, :] = nothing
                moduli[1, below, :] = nothing
            corners[turn, 1] = nothing[:XL]

        @pl.when(gx == GX - 1)
        def _():
            for n in range(3):
                v[n, above, :] = nothing
            if turn == 0:
                s_0[0, above, :] = nothing
                moduli[0, above, :] = nothing
                moduli[1, above, :] = nothing
            corners[turn, 0] = nothing[:XL]

        @pl.when(gy == 0)
        def _():
            for n in range(fields):
                receiving[0, n] = nothing[:XL]
            corners[turn, 0] = nothing[:XL]

        @pl.when(gy == GY - 1)
        def _():
            for n in range(fields):
                receiving[1, n] = nothing[:XL]
            corners[turn, 1] = nothing[:XL]

    def at_row(f, row):
        return lax.broadcasted_iota(jnp.int32, f.shape, 0) == row

    def at_lane(f, lane):
        return lax.broadcasted_iota(jnp.int32, f.shape, 1) == lane

    def next_z(f):
        return jnp.where(at_lane(f, NZ - 1), 0.0, pltpu.roll(f, NZ - 1, 1))

    def prior_z(f):
        return jnp.where(at_lane(f, 0), 0.0, pltpu.roll(f, 1, 1))

    def next_row(f, rim):
        return jnp.where(at_row(f, f.shape[0] - 1), rim, pltpu.roll(f, f.shape[0] - 1, 0))

    def prior_row(f, rim):
        return jnp.where(at_row(f, 0), rim, pltpu.roll(f, 1, 0))

    def plane_at(i):
        return i if isinstance(i, int) else pl.multiple_of(i, YL)

    def over_planes(plane):
        plane(0, False, True)

        def middle(i, carry):
            plane(i, True, True)
            return carry

        lax.fori_loop(1, XL - 1, middle, 0)
        plane(XL - 1, True, False)

    def stress_inside(v, s_in, s_out):
        def plane(i, has_before, has_after):
            here = pl.ds(plane_at((i + 1) * YL), YL)
            before = pl.ds(plane_at(i * YL), YL)
            after = pl.ds(plane_at((i + 2) * YL), YL)
            v_x, v_y, v_z = v[0, here, :], v[1, here, :], v[2, here, :]
            lam, mu = moduli[0, here, :], moduli[1, here, :]
            e_x = v_x - v[0, before, :] if has_before else v_x
            e_y = v_y - prior_row(v_y, 0.0)
            e_z = v_z - prior_z(v_z)
            x_y = v[1, after, :] - v_y if has_after else -v_y
            x_z = v[2, after, :] - v_z if has_after else -v_z
            volume = lam * (e_x + e_y + e_z)
            twice = 2.0 * mu
            s_out[0, here, :] = s_in[0, here, :] + (volume + twice * e_x)
            s_out[1, here, :] = s_in[1, here, :] + (volume + twice * e_y)
            s_out[2, here, :] = s_in[2, here, :] + (volume + twice * e_z)
            s_out[3, here, :] = s_in[3, here, :] + mu * ((next_row(v_x, 0.0) - v_x) + x_y)
            s_out[4, here, :] = s_in[4, here, :] + mu * ((next_z(v_x) - v_x) + x_z)
            s_out[5, here, :] = s_in[5, here, :] + mu * (
                (next_z(v_y) - v_y) + (next_row(v_z, 0.0) - v_z)
            )

        over_planes(plane)

    def stress_rims(v, s_in, s_out, received, turn):
        prior_side = [received[0, n] for n in range(3)]
        next_side = [received[1, n] for n in range(3)]
        corner_y = corners[turn, 0, pl.ds(0, 1), :]
        corner_x = corners[turn, 1, pl.ds(XL - 1, 1), :]

        gone = v[0, below, :]
        lam, mu = moduli[0, first, :], moduli[1, first, :]
        s_out[0, first, :] -= (lam + 2.0 * mu) * gone
        s_out[1, first, :] -= lam * gone
        s_out[2, first, :] -= lam * gone
        mu = moduli[1, last, :]
        s_out[3, last, :] += mu * v[1, above, :]
        s_out[4, last, :] += mu * v[2, above, :]

        gone = prior_side[1]
        lam, mu = moduli[0, top_rows, :], moduli[1, top_rows, :]
        s_out[0, top_rows, :] -= lam * gone
        s_out[1, top_rows, :] -= (lam + 2.0 * mu) * gone
        s_out[2, top_rows, :] -= lam * gone
        mu = moduli[1, end_rows, :]
        s_out[3, end_rows, :] += mu * next_side[0]
        s_out[5, end_rows, :] += mu * next_side[2]

        v_x, v_y, v_z = v[0, above, :], v[1, above, :], v[2, above, :]
        lam, mu = moduli[0, above, :], moduli[1, above, :]
        e_x = v_x - v[0, last, :]
        e_y = v_y - prior_row(v_y, corner_y)
        e_z = v_z - prior_z(v_z)
        s_out[0, above, :] = s_in[0, above, :] + (lam * (e_x + e_y + e_z) + 2.0 * mu * e_x)

        v_x, v_y, v_z = v[0, below, :], v[1, below, :], v[2, below, :]
        mu = moduli[1, below, :]
        s_out[3, below, :] = s_in[3, below, :] + mu * (
            (next_row(v_x, corner_x) - v_x) + (v[1, first, :] - v_y)
        )
        s_out[4, below, :] = s_in[4, below, :] + mu * (
            (next_z(v_x) - v_x) + (v[2, first, :] - v_z)
        )

        v_x, v_y, v_z = next_side
        lam, mu = y_recv[1, 4], y_recv[1, 5]
        e_x = v_x - prior_row(v_x, corner_x)
        e_y = v_y - v[1, end_rows, :]
        e_z = v_z - prior_z(v_z)
        old = y_recv[1, 3] if turn == 0 else rims[0]
        rims[0] = old + (lam * (e_x + e_y + e_z) + 2.0 * mu * e_y)

        v_x, v_y, v_z = prior_side
        mu = y_recv[0, 5]
        old = y_recv[0, 3] if turn == 0 else rims[1]
        rims[1] = old + mu * ((v[0, top_rows, :] - v_x) + (next_row(v_y, corner_y) - v_y))
        old = y_recv[0, 4] if turn == 0 else rims[2]
        rims[2] = old + mu * ((next_z(v_y) - v_y) + (v[2, top_rows, :] - v_z))

    def velocity_plane(v_in, s, v_out, i):
        here = pl.ds(plane_at((i + 1) * YL), YL)
        before = pl.ds(plane_at(i * YL), YL)
        after = pl.ds(plane_at((i + 2) * YL), YL)
        rim_yy, rim_xy, rim_yz = 0.0, 0.0, 0.0
        if isinstance(i, int):
            rim_yy, rim_xy, rim_yz = [rims[n, pl.ds(i, 1), :] for n in range(3)]
        b = moduli[2, here, :]
        xx, yy, zz = s[0, here, :], s[1, here, :], s[2, here, :]
        xy, xz, yz = s[3, here, :], s[4, here, :], s[5, here, :]
        v_out[0, here, :] = v_in[0, here, :] + b * (
            (s[0, after, :] - xx) + (xy - prior_row(xy, rim_xy)) + (xz - prior_z(xz))
        )
        v_out[1, here, :] = v_in[1, here, :] + b * (
            (xy - s[3, before, :]) + (next_row(yy, rim_yy) - yy) + (yz - prior_z(yz))
        )
        v_out[2, here, :] = v_in[2, here, :] + b * (
            (xz - s[4, before, :]) + (yz - prior_row(yz, rim_yz)) + (next_z(zz) - zz)
        )

    def velocity_inside(v_in, s, v_out):
        def middle(i, carry):
            velocity_plane(v_in, s, v_out, i)
            return carry

        lax.fori_loop(1, XL - 1, middle, 0)

    def velocity_rims(v_in, s, v_out):
        velocity_plane(v_in, s, v_out, 0)
        velocity_plane(v_in, s, v_out, XL - 1)
        for row in (0, YL - 1):
            rows = pl.ds(YL + row, XL, stride=YL)
            beside = pl.ds(YL + row + (1 if row == 0 else -1), XL, stride=YL)
            over, under = pl.ds(ROWS + YL + row, 1), pl.ds(row, 1)
            b = moduli[2, rows, :]
            xx, yy, zz = s[0, rows, :], s[1, rows, :], s[2, rows, :]
            xy, xz, yz = s[3, rows, :], s[4, rows, :], s[5, rows, :]
            if row == 0:
                xy_prior, yz_prior, yy_next = rims[1], rims[2], s[1, beside, :]
            else:
                xy_prior, yz_prior, yy_next = s[3, beside, :], s[5, beside, :], rims[0]
            v_out[0, rows, :] = v_in[0, rows, :] + b * (
                (next_row(xx, s[0, over, :]) - xx) + (xy - xy_prior) + (xz - prior_z(xz))
            )
            v_out[1, rows, :] = v_in[1, rows, :] + b * (
                (xy - prior_row(xy, s[3, under, :])) + (yy_next - yy) + (yz - prior_z(yz))
            )
            v_out[2, rows, :] = v_in[2, rows, :] + b * (
                (xz - prior_row(xz, s[4, under, :])) + (yz - yz_prior) + (next_z(zz) - zz)
            )

    wave_x = wave_x_of(0, iota(0))
    waves[0] = jnp.where(core == 0, wave_x, 1.0)
    waves[1], waves[2] = waves_here(place, column)

    @pl.when(core == 1)
    def _():
        x_recv[:, 1] = jnp.zeros((128, 4, 128), F32)

    for load in loads[:2]:
        load.wait()
    moduli[0, pl.ds(YL, ROWS), :] = lame_v[...].astype(F32) * time_step
    moduli[1, pl.ds(YL, ROWS), :] = shear_v[...].astype(F32) * time_step
    for load in loads[2:4]:
        load.wait()
    for side, rows in enumerate([end_rows, top_rows]):
        for n in range(3):
            y_send[side, n] = v_0[n, rows, :]
        y_send[side, 5] = moduli[1, rows, :]
    y_send[0, 3] = s_0[3, end_rows, :]
    y_send[0, 4] = s_0[5, end_rows, :]
    y_send[1, 3] = s_0[1, top_rows, :]
    y_send[1, 4] = moduli[0, top_rows, :]
    pl.semaphore_wait(barrier, 126 + 7 + 4)

    shears, both, only, one = pl.ds(3, 2), pl.ds(0, 2), pl.ds(0, 1), pl.ds(1, 1)
    copies = exchange(
        0,
        v_0,
        y_send,
        y_recv,
        [
            (s_0.at[shears, last], s_0.at[shears, below], (next_gx, gy)),
            (s_0.at[only, first], s_0.at[only, above], (prior_gx, gy)),
            (moduli.at[one, last], moduli.at[one, below], (next_gx, gy)),
            (moduli.at[both, first], moduli.at[both, above], (prior_gx, gy)),
        ],
    )
    stress_inside(v_0, s_0, s_1)
    loads[4].wait()
    moduli[2, pl.ds(YL, ROWS), :] = buoy_v[...].astype(F32) * time_step
    velocity_inside(v_0, s_1, v_1)
    arrive(0, copies, v_0, y_recv, 6)
    stress_rims(v_0, s_0, s_1, y_recv, 0)
    velocity_rims(v_0, s_1, v_1)
    for side, rows in enumerate([end_rows, top_rows]):
        for n in range(3):
            y_send_2[side, n] = v_1[n, rows, :]
    copies = exchange(1, v_1, y_send_2, y_recv_2, [])
    stress_inside(v_1, s_1, s_1)
    velocity_inside(v_1, s_1, v_2)
    arrive(1, copies, v_1, y_recv_2, 3)
    stress_rims(v_1, s_1, s_1, y_recv_2, 1)
    velocity_rims(v_1, s_1, v_2)

    for load in loads[5:8]:
        load.wait()

    def narrow(n):
        return small_v[n, 0], small_v[n, 1]

    def wide(n):
        return large_v[n, 0], large_v[n, 1]

    turn_y = turns_v[0], turns_v[1]
    turn_x = turns_v[2], turns_v[3]
    mine = gy % 2 * 64 + gx

    def landed(ref, sem):
        pltpu.make_async_copy(ref, ref, sem).wait()

    def planes_of(value):
        return [lanes(rows_of(value, part), h) for part in range(2) for h in range(2)]

    for n, plane in enumerate(planes_of(z_forward(v_2[1, pl.ds(YL, ROWS), :], narrow(0)))):
        z_one[:, n, :] = plane

    def send_one(k, carry):
        other, device = in_plane(k, 1)
        send(z_one.at[other], x_recv.at[mine, 0], device, one_send.at[0], plane_recv.at[0])
        return carry

    lax.fori_loop(1, 64, send_one, 0)

    for slot, field in enumerate([0, 2]):
        value = z_forward(v_2[field, pl.ds(YL, ROWS), :], narrow(slot))
        for n, plane in enumerate(planes_of(value)):
            z_two[:, slot, n, :] = plane

    def send_two(k, carry):
        other, device = in_plane(k, 0)
        send(z_two.at[other], x_recv.at[mine], device, two_send.at[0], plane_recv.at[0])
        return carry

    lax.fori_loop(1, 64, send_two, 0)

    @pl.when(core == 0)
    def _():
        send_one(0, 0)
        x_recv[mine] = z_two[column]

    @pl.when(core == 1)
    def _():
        send_two(0, 0)
        x_recv[mine, 0] = z_one[column]

    @pl.when(core == 0)
    def _():
        landed(x_recv.at[pl.ds(0, 127)], plane_recv.at[0])

    @pl.when(core == 1)
    def _():
        landed(x_recv.at[pl.ds(0, 127), 0], plane_recv.at[0])

    fields = [
        [x_recv[pl.ds(64 * z, 64), slot, n, :] for n in range(4)]
        for z in range(2)
        for slot in range(2)
    ]
    rows = x_forward(fields, narrow(4), *turn_x)
    alpha = waves[0]

    def ring_send_half(a, sending, receiving, turn):
        def one(k, carry):
            other, device = in_ring(k)
            send(
                sending.at[a, other],
                receiving.at[a, place],
                device,
                ring_send.at[turn, a],
                ring_recv.at[turn, a],
            )
            return carry

        lax.fori_loop(1, 8, one, 0)
        receiving[a, place] = sending[a, place]

    def ring_wait_half(a, receiving, turn):
        landed(receiving.at[a, pl.ds(0, 7)], ring_recv.at[turn, a])

    for a in range(2):
        got = matmul(rows[a], wide(2 + a))
        wave = lanes(alpha, a)
        for z in range(2):
            pair, other = rows_of(got, 2 * z), rows_of(got, 2 * z + 1)
            for part in range(2):
                value = wave * lanes(pair, part) + lanes(other, part)
                x_send[a, :, 2 * part + z] = value.reshape(8, 8, 128)
        ring_send_half(a, x_send, x_recv_2, 0)

    cosine, sine = [lanes(v, 0) for v in turn_y]
    for a in range(2):
        wave_y, inverse = lanes(waves[1], a), lanes(waves[2], a)
        ring_wait_half(a, x_recv_2, 0)
        arrived = [
            jnp.concatenate(
                [
                    x_recv_2[a, 2 * x + its_core, 2 * part + z]
                    for part in range(2)
                    for x in range(4)
                    for z in range(2)
                ],
                axis=0,
            )
            for its_core in range(2)
        ]
        out = matmul(narrow(2), jnp.concatenate(arrived, axis=1))
        stacked = []
        for n in range(2):
            block = lanes(out, n)
            stacked.append(
                jnp.concatenate(turned(block[:64], block[64:], cosine, sine, False), axis=1)
            )
        got = matmul(jnp.concatenate(stacked, axis=0), wide(0))
        wave = jnp.concatenate([wave_y, wave_y], axis=1)
        phi = (wave * rows_of(got, 1) + rows_of(got, 0)) * jnp.concatenate([inverse] * 2, axis=1)
        got = matmul(jnp.concatenate([phi, wave * phi], axis=0), wide(1))
        stacked = []
        for n in range(2):
            block = rows_of(got, n)
            stacked.append(
                jnp.concatenate(
                    turned(lanes(block, 0), lanes(block, 1), cosine, sine, True), axis=0
                )
            )
        out = matmul(narrow(3), jnp.concatenate(stacked, axis=1))
        for its_core in range(2):
            for part in range(2):
                for x in range(4):
                    for z in range(2):
                        row = part * 64 + (2 * x + z) * 8
                        x_send_2[a, 2 * x + its_core, 2 * part + z] = lanes(
                            out[row : row + 8], its_core
                        )
        ring_send_half(a, x_send_2, x_back, 1)

    def home(z, its_core, wide_one):
        def one(k, carry):
            chip = (gx // 2 + k) % 32
            device = (chip * 2 + its_core, gy // 2 * 2 + z)
            if wide_one:
                source = x_home.at[z * 64 + device[0]]
                send(source, z_two_back.at[column], device, two_send.at[1], plane_recv.at[1])
            else:
                source = x_home.at[z * 64 + device[0], 0]
                send(source, z_one_back.at[column], device, one_send.at[1], plane_recv.at[2])
            return carry

        return one

    products = []
    for a in range(2):
        ring_wait_half(a, x_back, 1)
        wave = jnp.concatenate([lanes(alpha, a)] * 2, axis=1)
        stacked = []
        for z in range(2):
            pair = [x_back[a, :, 2 * part + z].reshape(64, 128) for part in range(2)]
            pair = jnp.concatenate(pair, axis=1)
            stacked += [wave * pair, pair]
        products.append(matmul(jnp.concatenate(stacked, axis=0), wide(4 + a)))
    for z in range(2):
        zero, one = [v[128 * z : 128 * z + 128] for v in products]
        planes = x_backward(zero, one, narrow(5), *turn_x)
        for slot in range(2):
            for n in range(4):
                x_home[pl.ds(64 * z, 64), slot, n, :] = planes[slot][n]
        for its_core in range(2):

            @pl.when(core == its_core)
            def _():
                same, other = home(z, its_core, its_core == 0), home(z, 1 - its_core, its_core == 0)
                lax.fori_loop(1, 32, same, 0)
                lax.fori_loop(1, 32, other, 0)
                other(0, 0)

                @pl.when(gy % 2 != z)
                def _():
                    same(0, 0)

    @pl.when(core == 0)
    def _():
        z_two_back[column] = x_home[mine]

    @pl.when(core == 1)
    def _():
        z_one_back[column] = x_home[mine, 0]

    for load in loads[8:]:
        load.wait()

    def column_rows(planes):
        halves = [jnp.concatenate(planes[2 * p : 2 * p + 2], axis=1) for p in range(2)]
        return jnp.concatenate(halves, axis=0)

    total_p = jnp.zeros((ROWS, NZ), F32)
    total_s = jnp.zeros((ROWS, NZ), F32)
    for field in (1, 0, 2):
        if field == 1:

            @pl.when(core == 0)
            def _():
                landed(z_one_back, plane_recv.at[2])

            @pl.when(core == 1)
            def _():
                landed(z_one_back.at[pl.ds(0, 63)], plane_recv.at[2])

            planes = [z_one_back[:, n, :] for n in range(4)]
        else:
            if field == 0:

                @pl.when(core == 0)
                def _():
                    landed(z_two_back.at[pl.ds(0, 63)], plane_recv.at[1])

                @pl.when(core == 1)
                def _():
                    landed(z_two_back, plane_recv.at[1])

            planes = [z_two_back[:, field // 2, n, :] for n in range(4)]
        p_field = z_back(column_rows(planes), narrow(7 if field == 2 else 6))
        s_field = v_2[field, pl.ds(YL, ROWS), :] - p_field
        total_p += source_p_v[field].astype(F32) * p_field
        total_s += source_s_v[field].astype(F32) * s_field
    image_p[...] = total_p
    image_s[...] = total_s

    for copy in sent:
        copy.wait_send()
    for a in range(2):
        landed(x_send.at[a, pl.ds(0, 7)], ring_send.at[0, a])
        landed(x_send_2.at[a, pl.ds(0, 7)], ring_send.at[1, a])

    @pl.when(core == 0)
    def _():
        landed(z_two.at[pl.ds(0, 63)], two_send.at[0])
        landed(z_one, one_send.at[0])
        landed(x_home.at[pl.ds(0, 127)], two_send.at[1])

    @pl.when(core == 1)
    def _():
        landed(z_two, two_send.at[0])
        landed(z_one.at[pl.ds(0, 63)], one_send.at[0])
        landed(x_home.at[pl.ds(0, 127), 0], one_send.at[1])


def shards(small, large, turns, velocity, stress, lame, shear, buoy, source_p, source_s):
    in_place = pl.BlockSpec(memory_space=pltpu.HBM)
    padded = (XL + 2) * YL
    dma = pltpu.SemaphoreType.DMA
    scratch = [
        *[pltpu.VMEM((3, padded, NZ), F32)] * 3,
        *[pltpu.VMEM((6, padded, NZ), F32)] * 2,
        pltpu.VMEM((3, XL, NZ), F32),
        *[pltpu.VMEM((ROWS, NZ), BF16)] * 3,
        *[pltpu.VMEM((3, ROWS, NZ), BF16)] * 2,
        pltpu.VMEM(small.shape, BF16),
        pltpu.VMEM(large.shape, BF16),
        pltpu.VMEM(turns.shape, F32),
        pltpu.VMEM((3, padded, NZ), F32),
        *[pltpu.VMEM((2, 6, XL, NZ), F32)] * 2,
        *[pltpu.VMEM((2, 3, XL, NZ), F32)] * 2,
        pltpu.VMEM((2, 2, XL, NZ), F32),
        pltpu.VMEM((3, 64, 256), F32),
        pltpu.VMEM((64, 2, 4, 128), F32),
        pltpu.VMEM((64, 4, 128), F32),
        pltpu.VMEM((128, 2, 4, 128), F32),
        *[pltpu.VMEM((2, 8, 4, 8, 128), F32)] * 3,
        pltpu.VMEM((64, 2, 4, 128), F32),
        pltpu.VMEM((64, 4, 128), F32),
        pltpu.VMEM((2, 8, 4, 8, 128), F32),
        pltpu.VMEM((128, 2, 4, 128), F32),
        dma((10,)),
        dma((2, 10)),
        dma((2, 10)),
        dma((2,)),
        dma((2,)),
        dma((3,)),
        dma((2, 2)),
        dma((2, 2)),
    ]
    out = jax.ShapeDtypeStruct((ROWS, NZ), F32)
    outs = pl.pallas_call(
        kernel,
        out_shape=(out, out),
        in_specs=[in_place] * 10,
        out_specs=(pl.BlockSpec(memory_space=pltpu.VMEM),) * 2,
        scratch_shapes=scratch,
        compiler_params=pltpu.CompilerParams(
            collective_id=0, has_side_effects=True, vmem_limit_bytes=60 * 2**20
        ),
    )(
        velocity.reshape(3, ROWS, NZ),
        stress.reshape(6, ROWS, NZ),
        lame.reshape(ROWS, NZ),
        shear.reshape(ROWS, NZ),
        buoy.reshape(ROWS, NZ),
        source_p.reshape(3, ROWS, NZ),
        source_s.reshape(3, ROWS, NZ),
        small,
        large,
        turns,
    )
    return tuple(o.reshape(XL, YL, NZ) for o in outs)


def solution(mesh):
    small, large, turns = tables()

    def body(*blocks):
        return shards(jnp.asarray(small), jnp.asarray(large), jnp.asarray(turns), *blocks)

    in_specs = (
        P(None, "gx", "gy", None),
        P(None, "gx", "gy", None),
        P("gx", "gy", None),
        P("gx", "gy", None),
        P("gx", "gy", None),
        P(None, "gx", "gy", None),
        P(None, "gx", "gy", None),
    )
    out_specs = (P("gx", "gy", None), P("gx", "gy", None))
    return jax.shard_map(body, mesh=mesh, in_specs=in_specs, out_specs=out_specs, check_vma=False)
```

```python
import functools
import math

import jax
import jax.numpy as jnp
import numpy as np
from jax import lax
from jax.experimental import pallas as pl
from jax.experimental.pallas import tpu as pltpu
from jax.sharding import PartitionSpec as P

STEPS = 2
NX, NY, NZ = 512, 256, 128
GX, GY = 64, 8
XL, YL = NX // GX, NY // GY
ROWS = XL * YL
time_step = 0.2

MESH = pl.DeviceIdType.MESH
F32, BF16 = jnp.float32, jnp.bfloat16


def real_form(matrix):
    return np.block([[matrix.real, matrix.imag], [-matrix.imag, matrix.real]])


def left_form(matrix):
    return np.block([[matrix.real, -matrix.imag], [matrix.imag, matrix.real]])


def dft(length, sign):
    k = np.arange(length)
    return np.exp(sign * 2j * math.pi * (np.outer(k, k) % length) / length)


def tables():
    z = np.arange(NZ)
    forward_z = np.zeros((NZ, NZ))
    weighted_z = np.zeros((NZ, NZ))
    back_z = np.zeros((NZ, NZ))
    weighted_back = np.zeros((NZ, NZ))
    norm = 1.0 / (NX * NY * NZ)
    for column in range(NZ // 2):
        real_row, imag_row = column, NZ // 2 + column
        angle = 2 * math.pi * (column * z % NZ) / NZ
        cosine, sine = np.cos(angle), np.sin(angle)
        if column == 0:
            sign = 1.0 - 2.0 * (z % 2)
            forward_z[real_row], forward_z[imag_row] = 1.0, sign
            back_z[real_row], back_z[imag_row] = norm, norm * sign
        else:
            forward_z[real_row], forward_z[imag_row] = cosine, -sine
            back_z[real_row], back_z[imag_row] = 2 * norm * cosine, -2 * norm * sine
        weighted_z[real_row] = column * forward_z[real_row]
        weighted_z[imag_row] = column * forward_z[imag_row]
        weighted_back[real_row] = column * back_z[real_row]
        weighted_back[imag_row] = column * back_z[imag_row]

    per = NX // 64
    left_y = left_form(np.kron(dft(GY, -1), np.eye(per)))
    left_y_back = left_form(np.kron(dft(GY, 1), np.eye(per)))
    q1 = np.arange(64) // per
    yl = np.arange(ROWS) % YL
    turn_y = np.exp(-2j * math.pi * (np.outer(q1, yl) % NY) / NY)
    local_y = real_form(np.kron(np.eye(4), dft(YL, -1)))
    local_y_back = real_form(np.kron(np.eye(4), dft(YL, 1)))

    left_x = left_form(dft(GX, -1))
    left_x_back = left_form(dft(GX, 1))
    xl = np.arange(ROWS) // YL
    turn_x = np.exp(-2j * math.pi * (np.outer(np.arange(64), xl) % NX) / NX)
    local_x = []
    for a in range(2):
        small = np.diag(np.exp(-2j * math.pi * a * np.arange(4) / 8)) @ dft(4, -1)
        local_x.append(np.kron(small, np.eye(YL)))
    local_x_back = [real_form(m.conj().T) for m in local_x]
    local_x = [real_form(m) for m in local_x]

    def pair(stack):
        stack = np.stack(stack).astype(np.float32)
        high = stack.astype(BF16)
        low = (stack - high.astype(np.float32)).astype(BF16)
        return np.stack([high, low], axis=1)

    small = pair(
        [forward_z, weighted_z, left_y, left_y_back, left_x, left_x_back, back_z, weighted_back]
    )
    large = pair([local_y, local_y_back] + local_x + local_x_back)
    turns = np.stack([turn_y.real, turn_y.imag, turn_x.real, turn_x.imag]).astype(np.float32)
    return small, large, turns


def split(value):
    high = value.astype(BF16)
    return high, (value - high.astype(F32)).astype(BF16)


def product(left, right, dims):
    def one(a, b):
        return lax.dot_general(a, b, (dims, ((), ())), preferred_element_type=F32)

    return one(left[0], right[0]) + (one(left[0], right[1]) + one(left[1], right[0]))


NN = ((1,), (0,))
NT = ((1,), (1,))
TN = ((0,), (0,))


def matmul(left, right, dims=NN):
    left = left if isinstance(left, tuple) else split(left)
    right = right if isinstance(right, tuple) else split(right)
    return product(left, right, dims)


def turned(real, imag, cosine, sine, back):
    if back:
        return real * cosine + imag * sine, imag * cosine - real * sine
    return real * cosine - imag * sine, imag * cosine + real * sine


def lanes(value, half):
    return value[:, half * 128 : half * 128 + 128]


def z_forward(field, table):
    return matmul(table, field, NT)


def signed(positions, length):
    half = length // 2
    value = jnp.where(positions < half, positions, positions - length)
    return jnp.where(positions == half, 0, value).astype(F32)


def iota(axis):
    return lax.broadcasted_iota(jnp.int32, (64, 256), axis)


def wave_x_of(first, rows):
    lane = iota(1)
    return signed(first + rows + 64 * (lane // 128 + 2 * (lane % 128 // YL)), NX)


def waves_here(place, column):
    wave_x = wave_x_of(place * 8, iota(0) % 8)
    wave_y = signed(iota(0) // 8 + 8 * (iota(1) % YL), NY)
    wave_z = column.astype(F32)
    size = wave_x * wave_x + wave_y * wave_y + wave_z * wave_z
    return wave_y, 1.0 / jnp.maximum(size, 1.0)


def rows_of(value, n):
    return value[n * 64 : n * 64 + 64]


def x_forward(fields, left, cosine, sine):
    stacked = [
        jnp.concatenate([planes[h], planes[2 + h]], axis=0) for planes in fields for h in range(2)
    ]
    out = matmul(left, jnp.concatenate(stacked, axis=1))
    even, odd = [], []
    for n in range(len(fields)):
        block = out[:, n * 256 : n * 256 + 256]
        pair = turned(block[:64], block[64:], cosine, sine, False)
        even.append(jnp.concatenate([lanes(v, 0) + lanes(v, 1) for v in pair], axis=1))
        odd.append(jnp.concatenate([lanes(v, 0) - lanes(v, 1) for v in pair], axis=1))
    return [jnp.concatenate(v, axis=0) for v in (even, odd)]


def x_backward(zero, one, left, cosine, sine):
    count = zero.shape[0] // 64
    stacked = []
    for n in range(count):
        for h in range(2):
            even, odd = rows_of(zero, n), rows_of(one, n)
            both = even + odd if h == 0 else even - odd
            re, im = turned(
                lanes(both, 0), lanes(both, 1), lanes(cosine, h), lanes(sine, h), True
            )
            stacked.append(jnp.concatenate([re, im], axis=0))
    out = matmul(left, jnp.concatenate(stacked, axis=1))
    return [
        [lanes(rows_of(out, part), 2 * n + h) for part in range(2) for h in range(2)]
        for n in range(count)
    ]


def z_back(arrived, table):
    return matmul(arrived, table, TN)


def kernel(
    velocity, stress, lame, shear, buoy, source_p, source_s, small, large, turns,
    image_p, image_s,
    v_0, v_1, v_2, s_0, s_1, rims, lame_v, shear_v, buoy_v, source_p_v, source_s_v,
    small_v, large_v, turns_v, moduli, y_send, y_recv, y_send_2, y_recv_2, corners,
    waves, z_two, z_one, x_recv, x_send, x_recv_2, x_send_2, z_two_back, z_one_back,
    x_back, x_home, load_sem, halo_send, halo_recv,
    two_send, one_send, plane_recv, ring_send, ring_recv,
):
    gx, gy = lax.axis_index("gx"), lax.axis_index("gy")

    barrier = pltpu.get_barrier_semaphore()

    def greet(device):
        pl.semaphore_signal(barrier, inc=1, device_id=device, device_id_type=MESH)

    core, place = gx % 2, gy // 2 * 2 + gx % 2
    column = gy % 2 * 32 + gx // 2

    chip_0, row_0, own = gx // 2, gy // 2 * 2, gy % 2

    def over_plane(act):
        def far(k, carry):
            act(1 - own, lax.rem(chip_0 + k, 32))
            return carry

        def near(k, carry):
            act(own, lax.rem(chip_0 + k, 32))
            return carry

        lax.fori_loop(0, 32, far, 0)
        lax.fori_loop(1, 32, near, 0)

    def in_ring(k):
        other = (place + k) % 8
        return other, (gx // 2 * 2 + other % 2, other // 2 * 2 + gy % 2)

    def greet_plane(z, chip):
        greet((chip * 2, row_0 + z))
        greet((chip * 2 + 1, row_0 + z))

    def greet_ring(k, carry):
        greet(in_ring(k)[1])
        return carry

    next_gx, prior_gx = lax.rem(gx + 1, GX), lax.rem(gx + GX - 1, GX)
    next_gy, prior_gy = lax.rem(gy + 1, GY), lax.rem(gy + GY - 1, GY)
    def interior(ref):
        return ref.at[:, pl.ds(YL, ROWS)]

    loads = [
        (lame, lame_v),
        (shear, shear_v),
        (velocity, interior(v_0)),
        (stress, interior(s_0)),
        (buoy, buoy_v),
        (small, small_v),
        (large, large_v),
        (turns, turns_v),
        (source_p, source_p_v),
        (source_s, source_s_v),
    ]
    loads = [pltpu.make_async_copy(a, b, load_sem.at[n]) for n, (a, b) in enumerate(loads)]
    for load in loads:
        load.start()
    greet((gx, next_gy))
    greet((gx, prior_gy))
    greet((next_gx, prior_gy))
    greet((prior_gx, next_gy))
    over_plane(greet_plane)
    lax.fori_loop(1, 8, greet_ring, 0)

    def send(source, target, device, send_sem, recv_sem):
        copy = pltpu.make_async_remote_copy(
            src_ref=source,
            dst_ref=target,
            send_sem=send_sem,
            recv_sem=recv_sem,
            device_id=device,
            device_id_type=MESH,
        )
        copy.start()
        return copy

    first, last = pl.ds(YL, YL), pl.ds(ROWS, YL)
    below, above = pl.ds(0, YL), pl.ds(ROWS + YL, YL)
    top_rows = pl.ds(YL, XL, stride=YL)
    end_rows = pl.ds(2 * YL - 1, XL, stride=YL)
    every = pl.ds(0, 3)
    sent = []

    def exchange(turn, v, sending, receiving, more):
        plan = [
            (sending.at[0], receiving.at[0], (gx, next_gy)),
            (sending.at[1], receiving.at[1], (gx, prior_gy)),
            (sending.at[0, 1], corners.at[turn, 0], (prior_gx, next_gy)),
            (sending.at[1, 0], corners.at[turn, 1], (next_gx, prior_gy)),
            (v.at[every, last], v.at[every, below], (next_gx, gy)),
            (v.at[every, first], v.at[every, above], (prior_gx, gy)),
        ] + more
        copies = [
            send(source, target, device, halo_send.at[turn, n], halo_recv.at[turn, n])
            for n, (source, target, device) in enumerate(plan)
        ]
        sent.extend(copies)
        return copies

    def arrive(turn, copies, v, receiving, fields):
        for copy in copies:
            copy.wait_recv()
        nothing = jnp.zeros((YL, NZ), F32)

        @pl.when(gx == 0)
        def _():
            for n in range(3):
                v[n, below, :] = nothing
            if turn == 0:
                s_0[3, below, :] = nothing
                s_0[4, below, :] = nothing
                moduli[1, below, :] = nothing
            corners[turn, 1] = nothing[:XL]

        @pl.when(gx == GX - 1)
        def _():
            for n in range(3):
                v[n, above, :] = nothing
            if turn == 0:
                s_0[0, above, :] = nothing
                moduli[0, above, :] = nothing
                moduli[1, above, :] = nothing
            corners[turn, 0] = nothing[:XL]

        @pl.when(gy == 0)
        def _():
            for n in range(fields):
                receiving[0, n] = nothing[:XL]
            corners[turn, 0] = nothing[:XL]

        @pl.when(gy == GY - 1)
        def _():
            for n in range(fields):
                receiving[1, n] = nothing[:XL]
            corners[turn, 1] = nothing[:XL]

    def at_row(f, row):
        return lax.broadcasted_iota(jnp.int32, f.shape, 0) == row

    def at_lane(f, lane):
        return lax.broadcasted_iota(jnp.int32, f.shape, 1) == lane

    def next_z(f):
        return jnp.where(at_lane(f, NZ - 1), 0.0, pltpu.roll(f, NZ - 1, 1))

    def prior_z(f):
        return jnp.where(at_lane(f, 0), 0.0, pltpu.roll(f, 1, 1))

    def next_row(f, rim):
        return jnp.where(at_row(f, f.shape[0] - 1), rim, pltpu.roll(f, f.shape[0] - 1, 0))

    def prior_row(f, rim):
        return jnp.where(at_row(f, 0), rim, pltpu.roll(f, 1, 0))

    def plane_at(i):
        return i if isinstance(i, int) else pl.multiple_of(i, YL)

    def over_planes(plane):
        plane(0, False, True)

        def middle(i, carry):
            plane(i, True, True)
            return carry

        lax.fori_loop(1, XL - 1, middle, 0)
        plane(XL - 1, True, False)

    def stress_inside(v, s_in, s_out):
        def plane(i, has_before, has_after):
            here = pl.ds(plane_at((i + 1) * YL), YL)
            before = pl.ds(plane_at(i * YL), YL)
            after = pl.ds(plane_at((i + 2) * YL), YL)
            v_x, v_y, v_z = v[0, here, :], v[1, here, :], v[2, here, :]
            lam, mu = moduli[0, here, :], moduli[1, here, :]
            e_x = v_x - v[0, before, :] if has_before else v_x
            e_y = v_y - prior_row(v_y, 0.0)
            e_z = v_z - prior_z(v_z)
            x_y = v[1, after, :] - v_y if has_after else -v_y
            x_z = v[2, after, :] - v_z if has_after else -v_z
            volume = lam * (e_x + e_y + e_z)
            twice = 2.0 * mu
            s_out[0, here, :] = s_in[0, here, :] + (volume + twice * e_x)
            s_out[1, here, :] = s_in[1, here, :] + (volume + twice * e_y)
            s_out[2, here, :] = s_in[2, here, :] + (volume + twice * e_z)
            s_out[3, here, :] = s_in[3, here, :] + mu * ((next_row(v_x, 0.0) - v_x) + x_y)
            s_out[4, here, :] = s_in[4, here, :] + mu * ((next_z(v_x) - v_x) + x_z)
            s_out[5, here, :] = s_in[5, here, :] + mu * (
                (next_z(v_y) - v_y) + (next_row(v_z, 0.0) - v_z)
            )

        over_planes(plane)

    def stress_rims(v, s_in, s_out, received, turn):
        prior_side = [received[0, n] for n in range(3)]
        next_side = [received[1, n] for n in range(3)]
        corner_y = corners[turn, 0, pl.ds(0, 1), :]
        corner_x = corners[turn, 1, pl.ds(XL - 1, 1), :]

        gone = v[0, below, :]
        lam, mu = moduli[0, first, :], moduli[1, first, :]
        s_out[0, first, :] -= (lam + 2.0 * mu) * gone
        s_out[1, first, :] -= lam * gone
        s_out[2, first, :] -= lam * gone
        mu = moduli[1, last, :]
        s_out[3, last, :] += mu * v[1, above, :]
        s_out[4, last, :] += mu * v[2, above, :]

        gone = prior_side[1]
        lam, mu = moduli[0, top_rows, :], moduli[1, top_rows, :]
        s_out[0, top_rows, :] -= lam * gone
        s_out[1, top_rows, :] -= (lam + 2.0 * mu) * gone
        s_out[2, top_rows, :] -= lam * gone
        mu = moduli[1, end_rows, :]
        s_out[3, end_rows, :] += mu * next_side[0]
        s_out[5, end_rows, :] += mu * next_side[2]

        v_x, v_y, v_z = v[0, above, :], v[1, above, :], v[2, above, :]
        lam, mu = moduli[0, above, :], moduli[1, above, :]
        e_x = v_x - v[0, last, :]
        e_y = v_y - prior_row(v_y, corner_y)
        e_z = v_z - prior_z(v_z)
        s_out[0, above, :] = s_in[0, above, :] + (lam * (e_x + e_y + e_z) + 2.0 * mu * e_x)

        v_x, v_y, v_z = v[0, below, :], v[1, below, :], v[2, below, :]
        mu = moduli[1, below, :]
        s_out[3, below, :] = s_in[3, below, :] + mu * (
            (next_row(v_x, corner_x) - v_x) + (v[1, first, :] - v_y)
        )
        s_out[4, below, :] = s_in[4, below, :] + mu * (
            (next_z(v_x) - v_x) + (v[2, first, :] - v_z)
        )

        v_x, v_y, v_z = next_side
        lam, mu = y_recv[1, 4], y_recv[1, 5]
        e_x = v_x - prior_row(v_x, corner_x)
        e_y = v_y - v[1, end_rows, :]
        e_z = v_z - prior_z(v_z)
        old = y_recv[1, 3] if turn == 0 else rims[0]
        rims[0] = old + (lam * (e_x + e_y + e_z) + 2.0 * mu * e_y)

        v_x, v_y, v_z = prior_side
        mu = y_recv[0, 5]
        old = y_recv[0, 3] if turn == 0 else rims[1]
        rims[1] = old + mu * ((v[0, top_rows, :] - v_x) + (next_row(v_y, corner_y) - v_y))
        old = y_recv[0, 4] if turn == 0 else rims[2]
        rims[2] = old + mu * ((next_z(v_y) - v_y) + (v[2, top_rows, :] - v_z))

    def velocity_plane(v_in, s, v_out, i):
        here = pl.ds(plane_at((i + 1) * YL), YL)
        before = pl.ds(plane_at(i * YL), YL)
        after = pl.ds(plane_at((i + 2) * YL), YL)
        rim_yy, rim_xy, rim_yz = 0.0, 0.0, 0.0
        if isinstance(i, int):
            rim_yy, rim_xy, rim_yz = [rims[n, pl.ds(i, 1), :] for n in range(3)]
        b = moduli[2, here, :]
        xx, yy, zz = s[0, here, :], s[1, here, :], s[2, here, :]
        xy, xz, yz = s[3, here, :], s[4, here, :], s[5, here, :]
        v_out[0, here, :] = v_in[0, here, :] + b * (
            (s[0, after, :] - xx) + (xy - prior_row(xy, rim_xy)) + (xz - prior_z(xz))
        )
        v_out[1, here, :] = v_in[1, here, :] + b * (
            (xy - s[3, before, :]) + (next_row(yy, rim_yy) - yy) + (yz - prior_z(yz))
        )
        v_out[2, here, :] = v_in[2, here, :] + b * (
            (xz - s[4, before, :]) + (yz - prior_row(yz, rim_yz)) + (next_z(zz) - zz)
        )

    def velocity_inside(v_in, s, v_out):
        def middle(i, carry):
            velocity_plane(v_in, s, v_out, i)
            return carry

        lax.fori_loop(1, XL - 1, middle, 0)

    def velocity_rims(v_in, s, v_out):
        velocity_plane(v_in, s, v_out, 0)
        velocity_plane(v_in, s, v_out, XL - 1)
        for row in (0, YL - 1):
            rows = pl.ds(YL + row, XL, stride=YL)
            beside = pl.ds(YL + row + (1 if row == 0 else -1), XL, stride=YL)
            over, under = pl.ds(ROWS + YL + row, 1), pl.ds(row, 1)
            b = moduli[2, rows, :]
            xx, yy, zz = s[0, rows, :], s[1, rows, :], s[2, rows, :]
            xy, xz, yz = s[3, rows, :], s[4, rows, :], s[5, rows, :]
            if row == 0:
                xy_prior, yz_prior, yy_next = rims[1], rims[2], s[1, beside, :]
            else:
                xy_prior, yz_prior, yy_next = s[3, beside, :], s[5, beside, :], rims[0]
            v_out[0, rows, :] = v_in[0, rows, :] + b * (
                (next_row(xx, s[0, over, :]) - xx) + (xy - xy_prior) + (xz - prior_z(xz))
            )
            v_out[1, rows, :] = v_in[1, rows, :] + b * (
                (xy - prior_row(xy, s[3, under, :])) + (yy_next - yy) + (yz - prior_z(yz))
            )
            v_out[2, rows, :] = v_in[2, rows, :] + b * (
                (xz - prior_row(xz, s[4, under, :])) + (yz - yz_prior) + (next_z(zz) - zz)
            )

    wave_x = wave_x_of(0, iota(0))
    waves[0] = jnp.where(core == 0, wave_x, 1.0)
    waves[1], waves[2] = waves_here(place, column)

    @pl.when(core == 1)
    def _():
        x_recv[:, 1] = jnp.zeros((128, 4, 128), F32)

    for load in loads[:2]:
        load.wait()
    moduli[0, pl.ds(YL, ROWS), :] = lame_v[...].astype(F32) * time_step
    moduli[1, pl.ds(YL, ROWS), :] = shear_v[...].astype(F32) * time_step
    for load in loads[2:4]:
        load.wait()
    for side, rows in enumerate([end_rows, top_rows]):
        for n in range(3):
            y_send[side, n] = v_0[n, rows, :]
        y_send[side, 5] = moduli[1, rows, :]
    y_send[0, 3] = s_0[3, end_rows, :]
    y_send[0, 4] = s_0[5, end_rows, :]
    y_send[1, 3] = s_0[1, top_rows, :]
    y_send[1, 4] = moduli[0, top_rows, :]
    pl.semaphore_wait(barrier, 126 + 7 + 4)

    shears, both, only, one = pl.ds(3, 2), pl.ds(0, 2), pl.ds(0, 1), pl.ds(1, 1)
    copies = exchange(
        0,
        v_0,
        y_send,
        y_recv,
        [
            (s_0.at[shears, last], s_0.at[shears, below], (next_gx, gy)),
            (s_0.at[only, first], s_0.at[only, above], (prior_gx, gy)),
            (moduli.at[one, last], moduli.at[one, below], (next_gx, gy)),
            (moduli.at[both, first], moduli.at[both, above], (prior_gx, gy)),
        ],
    )
    stress_inside(v_0, s_0, s_1)
    loads[4].wait()
    moduli[2, pl.ds(YL, ROWS), :] = buoy_v[...].astype(F32) * time_step
    velocity_inside(v_0, s_1, v_1)
    arrive(0, copies, v_0, y_recv, 6)
    stress_rims(v_0, s_0, s_1, y_recv, 0)
    velocity_rims(v_0, s_1, v_1)
    for side, rows in enumerate([end_rows, top_rows]):
        for n in range(3):
            y_send_2[side, n] = v_1[n, rows, :]
    copies = exchange(1, v_1, y_send_2, y_recv_2, [])
    stress_inside(v_1, s_1, s_1)
    velocity_inside(v_1, s_1, v_2)
    arrive(1, copies, v_1, y_recv_2, 3)
    stress_rims(v_1, s_1, s_1, y_recv_2, 1)
    velocity_rims(v_1, s_1, v_2)

    for load in loads[5:8]:
        load.wait()

    def narrow(n):
        return small_v[n, 0], small_v[n, 1]

    def wide(n):
        return large_v[n, 0], large_v[n, 1]

    turn_y = turns_v[0], turns_v[1]
    turn_x = turns_v[2], turns_v[3]
    mine = gy % 2 * 64 + gx

    def landed(ref, sem):
        pltpu.make_async_copy(ref, ref, sem).wait()

    def planes_of(value):
        return [lanes(rows_of(value, part), h) for part in range(2) for h in range(2)]

    for n, plane in enumerate(planes_of(z_forward(v_2[1, pl.ds(YL, ROWS), :], narrow(0)))):
        z_one[:, n, :] = plane

    def send_one(z, chip):
        device = (chip * 2 + 1, row_0 + z)
        source = z_one.at[z * 32 + chip]
        send(source, x_recv.at[mine, 0], device, one_send.at[0], plane_recv.at[0])

    over_plane(send_one)

    for slot, field in enumerate([0, 2]):
        value = z_forward(v_2[field, pl.ds(YL, ROWS), :], narrow(slot))
        for n, plane in enumerate(planes_of(value)):
            z_two[:, slot, n, :] = plane

    def send_two(z, chip):
        device = (chip * 2, row_0 + z)
        source = z_two.at[z * 32 + chip]
        send(source, x_recv.at[mine], device, two_send.at[0], plane_recv.at[0])

    over_plane(send_two)

    @pl.when(core == 0)
    def _():
        send_one(own, chip_0)
        x_recv[mine] = z_two[column]

    @pl.when(core == 1)
    def _():
        send_two(own, chip_0)
        x_recv[mine, 0] = z_one[column]

    @pl.when(core == 0)
    def _():
        landed(x_recv.at[pl.ds(0, 127)], plane_recv.at[0])

    @pl.when(core == 1)
    def _():
        landed(x_recv.at[pl.ds(0, 127), 0], plane_recv.at[0])

    fields = [
        [x_recv[pl.ds(64 * z, 64), slot, n, :] for n in range(4)]
        for z in range(2)
        for slot in range(2)
    ]
    rows = x_forward(fields, narrow(4), *turn_x)
    alpha = waves[0]

    def ring_send_half(a, sending, receiving, turn):
        def one(k, carry):
            other, device = in_ring(k)
            send(
                sending.at[a, other],
                receiving.at[a, place],
                device,
                ring_send.at[turn, a],
                ring_recv.at[turn, a],
            )
            return carry

        lax.fori_loop(1, 8, one, 0)
        receiving[a, place] = sending[a, place]

    def ring_wait_half(a, receiving, turn):
        landed(receiving.at[a, pl.ds(0, 7)], ring_recv.at[turn, a])

    for a in range(2):
        got = matmul(rows[a], wide(2 + a))
        wave = lanes(alpha, a)
        for z in range(2):
            pair, other = rows_of(got, 2 * z), rows_of(got, 2 * z + 1)
            for part in range(2):
                value = wave * lanes(pair, part) + lanes(other, part)
                x_send[a, :, 2 * part + z] = value.reshape(8, 8, 128)
        ring_send_half(a, x_send, x_recv_2, 0)

    cosine, sine = [lanes(v, 0) for v in turn_y]
    for a in range(2):
        wave_y, inverse = lanes(waves[1], a), lanes(waves[2], a)
        ring_wait_half(a, x_recv_2, 0)
        arrived = [
            jnp.concatenate(
                [
                    x_recv_2[a, 2 * x + its_core, 2 * part + z]
                    for part in range(2)
                    for x in range(4)
                    for z in range(2)
                ],
                axis=0,
            )
            for its_core in range(2)
        ]
        out = matmul(narrow(2), jnp.concatenate(arrived, axis=1))
        stacked = []
        for n in range(2):
            block = lanes(out, n)
            stacked.append(
                jnp.concatenate(turned(block[:64], block[64:], cosine, sine, False), axis=1)
            )
        got = matmul(jnp.concatenate(stacked, axis=0), wide(0))
        wave = jnp.concatenate([wave_y, wave_y], axis=1)
        phi = (wave * rows_of(got, 1) + rows_of(got, 0)) * jnp.concatenate([inverse] * 2, axis=1)
        got = matmul(jnp.concatenate([phi, wave * phi], axis=0), wide(1))
        stacked = []
        for n in range(2):
            block = rows_of(got, n)
            stacked.append(
                jnp.concatenate(
                    turned(lanes(block, 0), lanes(block, 1), cosine, sine, True), axis=0
                )
            )
        out = matmul(narrow(3), jnp.concatenate(stacked, axis=1))
        for its_core in range(2):
            for part in range(2):
                for x in range(4):
                    for z in range(2):
                        row = part * 64 + (2 * x + z) * 8
                        x_send_2[a, 2 * x + its_core, 2 * part + z] = lanes(
                            out[row : row + 8], its_core
                        )
        ring_send_half(a, x_send_2, x_back, 1)

    def home(z, its_core, wide_one):
        def one(k, carry):
            chip = lax.rem(chip_0 + k, 32)
            device = (chip * 2 + its_core, row_0 + z)
            if wide_one:
                source = x_home.at[z * 64 + device[0]]
                send(source, z_two_back.at[column], device, two_send.at[1], plane_recv.at[1])
            else:
                source = x_home.at[z * 64 + device[0], 0]
                send(source, z_one_back.at[column], device, one_send.at[1], plane_recv.at[2])
            return carry

        return one

    products = []
    for a in range(2):
        ring_wait_half(a, x_back, 1)
        wave = jnp.concatenate([lanes(alpha, a)] * 2, axis=1)
        stacked = []
        for z in range(2):
            pair = [x_back[a, :, 2 * part + z].reshape(64, 128) for part in range(2)]
            pair = jnp.concatenate(pair, axis=1)
            stacked += [wave * pair, pair]
        products.append(matmul(jnp.concatenate(stacked, axis=0), wide(4 + a)))
    for z in range(2):
        zero, one = [v[128 * z : 128 * z + 128] for v in products]
        planes = x_backward(zero, one, narrow(5), *turn_x)
        for slot in range(2):
            for n in range(4):
                x_home[pl.ds(64 * z, 64), slot, n, :] = planes[slot][n]
        for its_core in range(2):

            @pl.when(core == its_core)
            def _():
                same, other = home(z, its_core, its_core == 0), home(z, 1 - its_core, its_core == 0)
                lax.fori_loop(1, 32, same, 0)
                lax.fori_loop(1, 32, other, 0)
                other(0, 0)

                @pl.when(gy % 2 != z)
                def _():
                    same(0, 0)

    @pl.when(core == 0)
    def _():
        z_two_back[column] = x_home[mine]

    @pl.when(core == 1)
    def _():
        z_one_back[column] = x_home[mine, 0]

    for load in loads[8:]:
        load.wait()

    def column_rows(planes):
        halves = [jnp.concatenate(planes[2 * p : 2 * p + 2], axis=1) for p in range(2)]
        return jnp.concatenate(halves, axis=0)

    total_p = jnp.zeros((ROWS, NZ), F32)
    total_s = jnp.zeros((ROWS, NZ), F32)
    for field in (1, 0, 2):
        if field == 1:

            @pl.when(core == 0)
            def _():
                landed(z_one_back, plane_recv.at[2])

            @pl.when(core == 1)
            def _():
                landed(z_one_back.at[pl.ds(0, 63)], plane_recv.at[2])

            planes = [z_one_back[:, n, :] for n in range(4)]
        else:
            if field == 0:

                @pl.when(core == 0)
                def _():
                    landed(z_two_back.at[pl.ds(0, 63)], plane_recv.at[1])

                @pl.when(core == 1)
                def _():
                    landed(z_two_back, plane_recv.at[1])

            planes = [z_two_back[:, field // 2, n, :] for n in range(4)]
        p_field = z_back(column_rows(planes), narrow(7 if field == 2 else 6))
        s_field = v_2[field, pl.ds(YL, ROWS), :] - p_field
        total_p += source_p_v[field].astype(F32) * p_field
        total_s += source_s_v[field].astype(F32) * s_field
    image_p[...] = total_p
    image_s[...] = total_s

    for copy in sent:
        copy.wait_send()
    for a in range(2):
        landed(x_send.at[a, pl.ds(0, 7)], ring_send.at[0, a])
        landed(x_send_2.at[a, pl.ds(0, 7)], ring_send.at[1, a])

    @pl.when(core == 0)
    def _():
        landed(z_two.at[pl.ds(0, 63)], two_send.at[0])
        landed(z_one, one_send.at[0])
        landed(x_home.at[pl.ds(0, 127)], two_send.at[1])

    @pl.when(core == 1)
    def _():
        landed(z_two, two_send.at[0])
        landed(z_one.at[pl.ds(0, 63)], one_send.at[0])
        landed(x_home.at[pl.ds(0, 127), 0], one_send.at[1])


def shards(small, large, turns, velocity, stress, lame, shear, buoy, source_p, source_s):
    in_place = pl.BlockSpec(memory_space=pltpu.HBM)
    padded = (XL + 2) * YL
    dma = pltpu.SemaphoreType.DMA
    scratch = [
        *[pltpu.VMEM((3, padded, NZ), F32)] * 3,
        *[pltpu.VMEM((6, padded, NZ), F32)] * 2,
        pltpu.VMEM((3, XL, NZ), F32),
        *[pltpu.VMEM((ROWS, NZ), BF16)] * 3,
        *[pltpu.VMEM((3, ROWS, NZ), BF16)] * 2,
        pltpu.VMEM(small.shape, BF16),
        pltpu.VMEM(large.shape, BF16),
        pltpu.VMEM(turns.shape, F32),
        pltpu.VMEM((3, padded, NZ), F32),
        *[pltpu.VMEM((2, 6, XL, NZ), F32)] * 2,
        *[pltpu.VMEM((2, 3, XL, NZ), F32)] * 2,
        pltpu.VMEM((2, 2, XL, NZ), F32),
        pltpu.VMEM((3, 64, 256), F32),
        pltpu.VMEM((64, 2, 4, 128), F32),
        pltpu.VMEM((64, 4, 128), F32),
        pltpu.VMEM((128, 2, 4, 128), F32),
        *[pltpu.VMEM((2, 8, 4, 8, 128), F32)] * 3,
        pltpu.VMEM((64, 2, 4, 128), F32),
        pltpu.VMEM((64, 4, 128), F32),
        pltpu.VMEM((2, 8, 4, 8, 128), F32),
        pltpu.VMEM((128, 2, 4, 128), F32),
        dma((10,)),
        dma((2, 10)),
        dma((2, 10)),
        dma((2,)),
        dma((2,)),
        dma((3,)),
        dma((2, 2)),
        dma((2, 2)),
    ]
    out = jax.ShapeDtypeStruct((ROWS, NZ), F32)
    outs = pl.pallas_call(
        kernel,
        out_shape=(out, out),
        in_specs=[in_place] * 10,
        out_specs=(pl.BlockSpec(memory_space=pltpu.VMEM),) * 2,
        scratch_shapes=scratch,
        compiler_params=pltpu.CompilerParams(
            collective_id=0, has_side_effects=True, vmem_limit_bytes=60 * 2**20
        ),
    )(
        velocity.reshape(3, ROWS, NZ),
        stress.reshape(6, ROWS, NZ),
        lame.reshape(ROWS, NZ),
        shear.reshape(ROWS, NZ),
        buoy.reshape(ROWS, NZ),
        source_p.reshape(3, ROWS, NZ),
        source_s.reshape(3, ROWS, NZ),
        small,
        large,
        turns,
    )
    return tuple(o.reshape(XL, YL, NZ) for o in outs)


def solution(mesh):
    small, large, turns = tables()

    def body(*blocks):
        return shards(jnp.asarray(small), jnp.asarray(large), jnp.asarray(turns), *blocks)

    in_specs = (
        P(None, "gx", "gy", None),
        P(None, "gx", "gy", None),
        P("gx", "gy", None),
        P("gx", "gy", None),
        P("gx", "gy", None),
        P(None, "gx", "gy", None),
        P(None, "gx", "gy", None),
    )
    out_specs = (P("gx", "gy", None), P("gx", "gy", None))
    return jax.shard_map(body, mesh=mesh, in_specs=in_specs, out_specs=out_specs, check_vma=False)
```
